32 devices in a mesh: grp: 4 (over y, x), dev: 8 (over z, core).
Axes of the slice: x: 2, y: 2, z: 4, core: 2. Of those that a mesh axis runs over, the one named last changes fastest.
Arguments:
- raw: bfloat16 [128, 16, 4096], P(('grp', 'dev'))
- dark: bfloat16 [16, 4096], replicated, may hold values from 0.049804688 to 0.29882812
- basis: bfloat16 [8, 4096], replicated, may hold values from -3 to 3
- counts: int32 [128], P(('grp', 'dev')), may hold values from 1 to 16, as said below
- positions: int32 [128], replicated, may hold values from 0 to 127, as said below
Outputs:
- corrected: bfloat16 [128, 16, 4096], P(('grp', 'dev'))
- pooled: bfloat16 [4, 16, 1, 30720], P('grp', None, None, 'dev')
The draws below stay inside these ranges and needn't reach their ends.
Inputs may be any that keep to these rules, and one draw needn't show every extreme that they name: `counts`: the first tile of every device (4 tiles in acquisition order) has all 16 planes. A permutation of the tile positions of the slide image. The 4 tiles of the device at grp index g and dev index d lie in 4 different bands, all at tile columns d * 4 to d * 4 + 3.
All inputs are finite; a program needn't handle non-finite values.
Results may differ from the reference program's by a relative error of at most 0.0046.
Values may be sent and summed in bfloat16 or wider, within the bound.
A program may use at most 128 MiB of HBM per device.

```python
import jax
import jax.numpy as jnp
from jax import lax

ROWS = 2
COLS = 2048
OVL = 128
PLANES = 16
RANK = 8
TILES_DEV = 4
TILES = 128
PIX = 4096
BAND = 32
N_GRP = 4
N_DEV = 8


def shading_parts(key):
    basis_key = jax.random.fold_in(key, 11)
    basis = jnp.clip(jax.random.normal(basis_key, (RANK, PIX), jnp.float32), -3.0, 3.0)
    weights = jax.random.normal(jax.random.fold_in(key, 12), (RANK, PLANES), jnp.float32) * 0.1
    drift = jax.random.normal(jax.random.fold_in(key, 13), (RANK, PLANES), jnp.float32) * 0.15
    blocks = TILES // TILES_DEV
    offsets = jax.random.normal(jax.random.fold_in(key, 14), (blocks, RANK, PLANES), jnp.float32) * 0.3
    return (basis, weights, drift, offsets)


def draw_basis(key, part):
    basis, weights, drift, offsets = shading_parts(key)
    return basis.astype(jnp.bfloat16)


def draw_raw(key, part):
    basis, weights, drift, offsets = shading_parts(key)
    blocks = TILES // TILES_DEV
    order = jnp.arange(TILES, dtype=jnp.float32) / TILES
    block_of = jnp.arange(TILES, dtype=jnp.int32) // TILES_DEV
    tile_weights = weights[None] + order[:, None, None] * drift[None] + offsets[block_of]
    shade = jnp.einsum('tkp,kx->tpx', tile_weights, basis)
    block_bright = jnp.exp(jax.random.uniform(jax.random.fold_in(key, 23), (blocks,), jnp.float32, jnp.log(0.3), jnp.log(3.0)))
    rough = jax.random.uniform(jax.random.fold_in(key, 22), (TILES, PLANES, PIX), jnp.float32, 0.5, 1.5)
    bright = 0.4 * jnp.exp(jnp.log(3.0) * order) * jax.random.uniform(jax.random.fold_in(key, 21), (TILES,), jnp.float32, 0.7, 1.4)
    bright = bright * block_bright[block_of]
    values = 0.36 + bright[:, None, None] * rough * jnp.exp(shade)
    return values.astype(jnp.bfloat16)


def draw_counts(key, part):
    drawn = jax.random.randint(jax.random.fold_in(key, 31), (TILES,), 1, PLANES + 1)
    first = jnp.arange(TILES, dtype=jnp.int32) % TILES_DEV == 0
    return jnp.where(first, PLANES, drawn).astype(jnp.int32)


def draw_positions(key, part):
    sources = N_GRP * N_DEV
    band_keys = jax.random.split(jax.random.fold_in(key, 41), sources)
    bands = jax.vmap(lambda k: jax.random.permutation(k, N_GRP))(band_keys).reshape(N_GRP, N_DEV, TILES_DEV)
    slot_keys = jax.random.split(jax.random.fold_in(key, 42), sources)
    slots = jax.vmap(lambda k: jax.random.permutation(k, N_GRP))(slot_keys).reshape(N_GRP, N_DEV, N_GRP)
    column_ids = jnp.arange(N_DEV, dtype=jnp.int32)[None, :, None]
    source_ids = jnp.arange(N_GRP, dtype=jnp.int32)[:, None, None]
    slot = slots[bands, column_ids, source_ids]
    places = bands * BAND + column_ids * TILES_DEV + slot
    return places.reshape(TILES).astype(jnp.int32)


def setup_inputs(seed: int = 0) -> dict:
    key_list = jax.random.split(jax.random.key(seed), 6)
    raw = draw_raw(jax.random.fold_in(key_list[5], 71), 0)
    dark = jnp.clip(jax.random.uniform(key_list[1], (PLANES, PIX), jnp.float32, 0.049804688, 0.29882812), 0.049804688, 0.29882812).astype(jnp.bfloat16)
    basis = draw_basis(jax.random.fold_in(key_list[5], 71), 0)
    counts = draw_counts(jax.random.fold_in(key_list[5], 71), 0)
    positions = draw_positions(jax.random.fold_in(key_list[5], 71), 0)
    return {"raw": raw, "dark": dark, "basis": basis, "counts": counts, "positions": positions}


def feather():
    column = jnp.arange(COLS, dtype=jnp.float32) + 0.5
    return jnp.minimum(1.0, jnp.minimum(column / OVL, (COLS - column) / OVL))


def pooling(tiles):
    count = tiles.shape[0]
    shaped = tiles.reshape(count, PLANES, ROWS, COLS) * feather()
    return jnp.sum(shaped.reshape(count, PLANES, ROWS // 2, 2, COLS // 2, 2), axis=(3, 5)) * 0.25


def reference(raw, dark, basis, counts, positions):
    live = (jnp.arange(PLANES, dtype=jnp.int32)[None, :] < counts[:, None]).astype(jnp.float32)
    blocks = TILES // TILES_DEV
    raw_blocks = raw.reshape(blocks, TILES_DEV, PLANES, PIX)
    live_blocks = live.reshape(blocks, TILES_DEV, PLANES)
    basis_f = basis.astype(jnp.float32)
    dark_f = dark.astype(jnp.float32)

    def gather_terms(carry, item):
        tiles, alive = item
        tiles_f = tiles.astype(jnp.float32)
        projected = jnp.einsum("kx,tpx->tkp", basis_f, tiles_f)
        local_proj = jnp.sum(projected * alive[:, None, :], axis=0)
        local_sum = jnp.sum(jnp.sum(tiles_f, axis=2) * alive, axis=0)
        return (carry[0] + local_proj, carry[1] + local_sum, carry[2] + jnp.sum(alive, axis=0)), None

    start = (jnp.zeros((RANK, PLANES), jnp.float32), jnp.zeros((PLANES,), jnp.float32), jnp.zeros((PLANES,), jnp.float32))
    (proj, total, alive), _ = lax.scan(gather_terms, start, (raw_blocks, live_blocks))
    dark_proj = jnp.dot(basis, dark.T, preferred_element_type=jnp.float32)
    dark_sum = jnp.sum(dark_f, axis=1)
    coef = (proj - alive[None, :] * dark_proj) / (total - alive * dark_sum)[None, :]
    shade = jnp.dot(coef.T, basis_f, precision=lax.Precision.HIGHEST)
    inverse = jnp.exp(-shade)

    def repair(item):
        tiles, alive_rows = item
        return ((tiles.astype(jnp.float32) - dark_f[None]) * inverse[None] * alive_rows[:, :, None]).astype(jnp.bfloat16)

    corrected = lax.map(repair, (raw_blocks, live_blocks)).reshape(TILES, PLANES, PIX)
    order = jnp.argsort(positions).astype(jnp.int32)
    half_step = (COLS - OVL) // 2
    half_ovl = OVL // 2

    def band_rows(band):
        chosen = lax.dynamic_slice_in_dim(order, band * BAND, BAND)
        cells = pooling(corrected[chosen].astype(jnp.float32)).astype(jnp.bfloat16)
        cells = lax.optimization_barrier(cells)
        head = cells[..., :half_step].astype(jnp.float32)
        tail = cells[..., half_step:]
        carried = jnp.concatenate([jnp.zeros_like(tail[:1]), tail[:-1]], axis=0)
        carried = jnp.pad(carried, ((0, 0), (0, 0), (0, 0), (0, half_step - half_ovl))).astype(jnp.float32)
        merged = head + carried
        return jnp.transpose(merged, (1, 2, 0, 3)).reshape(PLANES, ROWS // 2, BAND * half_step).astype(jnp.bfloat16)

    pooled = lax.map(band_rows, jnp.arange(N_GRP, dtype=jnp.int32))
    return corrected, pooled
```

```python
import functools

import jax
import jax.numpy as jnp
from jax import lax
from jax.experimental import pallas as pl
from jax.experimental.pallas import tpu as pltpu
from jax.sharding import PartitionSpec as P

ROWS = 2
COLS = 2048
OVL = 128
LANES = 128
BLOCK = 256
PAIR = 2
MESH = pl.DeviceIdType.MESH
NT = (((1,), (1,)), ((), ()))


def pick(options):
    found = jnp.int32(0)
    for hit, value in options:
        found = jnp.where(hit, value, found)
    return found


def pool_weights(start):
    row = lax.broadcasted_iota(jnp.int32, (BLOCK, LANES), 0)
    lane = lax.broadcasted_iota(jnp.int32, (BLOCK, LANES), 1)
    column = (row + start).astype(jnp.float32) + 0.5
    ramp = jnp.minimum(1.0, jnp.minimum(column / OVL, (COLS - column) / OVL))
    inside = (row >= 2 * lane) & (row < 2 * lane + 2)
    return jnp.where(inside, 0.25 * jnp.maximum(ramp, 0.0), 0.0).astype(jnp.bfloat16)


STARTS = (0, BLOCK, COLS - BLOCK, -OVL, COLS - OVL)


def gather(
    groups, columns,
    counts_hbm, positions_hbm, raw_hbm, dark_hbm, basis_hbm,
    own_ref, came_ref, spill_ref, sums_ref, stack_ref, weights_ref,
    counts_ref, positions_ref, raw_ref, dark_ref, rhs, stat, mine, inbox, outgoing, arrived, tail_out, tail_in,
    in_sem, raw_sem, above, stat_send, stat_recv, cell_send, cell_recv, tail_send, tail_recv,
):
    tiles, planes, pixels = raw_ref.shape
    rank = basis_hbm.shape[0]
    band_size = columns * tiles
    devices = groups * columns
    chunks = raw_sem.shape[0]
    chunk = pixels // chunks
    g = lax.axis_index("grp")
    d = lax.axis_index("dev")
    first = lax.div(d, PAIR) * PAIR
    me = d * groups + g

    loads = [
        pltpu.make_async_copy(basis_hbm, rhs.at[0:rank], in_sem.at[0]),
        pltpu.make_async_copy(dark_hbm, dark_ref, in_sem.at[1]),
        pltpu.make_async_copy(counts_hbm, counts_ref, in_sem.at[2]),
        pltpu.make_async_copy(positions_hbm, positions_ref, in_sem.at[3]),
    ]
    raw_loads = [
        pltpu.make_async_copy(
            raw_hbm.at[:, :, c * chunk:(c + 1) * chunk], raw_ref.at[:, :, c * chunk:(c + 1) * chunk],
            raw_sem.at[c],
        ) for c in range(chunks)
    ]
    for copy in loads[:2] + raw_loads + loads[2:]:
        copy.start()

    barrier = pltpu.get_barrier_semaphore()
    layer = [
        (lax.rem(g + a, groups), first + lax.rem(d - first + b, PAIR))
        for b in range(PAIR) for a in range(groups) if a or b
    ]
    for where in layer:
        pl.semaphore_signal(barrier, inc=1, device_id=where, device_id_type=MESH)

    @pl.loop(first + PAIR, columns)
    def _(column):
        for a in range(groups):
            pl.semaphore_signal(
                barrier, inc=1, device_id=(jnp.int32(a), column), device_id_type=MESH
            )

    pl.semaphore_wait(barrier, (first + PAIR) * groups - 1)

    @pl.loop(0, first)
    def _(column):
        for a in range(groups):
            pl.semaphore_signal(above, inc=1, device_id=(jnp.int32(a), column), device_id_type=MESH)

    rhs[rank:, :] = jnp.ones((rhs.shape[0] - rank, pixels), jnp.bfloat16)
    width = rhs.shape[0]
    stat[...] = jnp.zeros_like(stat)
    for copy in loads:
        copy.wait()
    sums = jnp.zeros(((tiles + 1) * planes, width), jnp.float32)
    for c in range(chunks):
        raw_loads[c].wait()
        span = slice(c * chunk, (c + 1) * chunk)
        lhs = jnp.concatenate(
            [raw_ref[:, :, span].reshape(tiles * planes, chunk), dark_ref[:, span]], axis=0
        )
        sums = sums + lax.dot_general(lhs, rhs[:, span], NT, preferred_element_type=jnp.float32)
    dark_sums = sums[tiles * planes:]
    plane = lax.broadcasted_iota(jnp.int32, (planes, width), 0)
    local = jnp.zeros((planes, width), jnp.float32)
    for t in range(tiles):
        part = sums[t * planes:(t + 1) * planes] - dark_sums
        local = local + jnp.where(plane < counts_ref[t], part, 0.0)
    stat[:, 0:width] = local
    lane = lax.broadcasted_iota(jnp.int32, (planes, LANES), 1)
    for i, turned in enumerate((stat[...], pltpu.roll(stat[...], LANES - rank, 1))):
        kept = jnp.where(lane < rank, turned, 0.0)
        spread = pltpu.roll(kept, 0, 1, stride=rank, stride_axis=0)
        mine[i:i + 1, :] = jnp.sum(spread, axis=0, keepdims=True)

    def stat_copy(a, column):
        slot = lax.rem(me - (column * groups + a) + devices, devices) - 1
        return pltpu.make_async_remote_copy(
            src_ref=mine, dst_ref=inbox.at[slot], send_sem=stat_send, recv_sem=stat_recv,
            device_id=(a, column), device_id_type=MESH,
        )

    @pl.loop(0, first)
    def _(column):
        for a in range(groups):
            stat_copy(jnp.int32(a), column).start()

    for a, column in layer:
        stat_copy(a, column).start()

    def home(at):
        return lax.div(at, band_size), lax.rem(at, tiles)

    wide = lax.broadcasted_iota(jnp.int32, (planes, pixels), 0)
    mine_home = [home(positions_ref[(g * columns + d) * tiles + t]) for t in range(tiles)]

    def build(b):
        chosen = pick((mine_home[t][0] == b, t) for t in range(tiles))
        masked = jnp.where(
            wide < counts_ref[chosen],
            raw_ref[chosen].astype(jnp.float32), dark_ref[...].astype(jnp.float32),
        ).astype(jnp.bfloat16)
        outgoing[b] = masked
        for row in range(ROWS):
            tail_out[b, row] = masked[:, (row + 1) * COLS - OVL:(row + 1) * COLS]

    others = [jnp.where(g <= o, o + 1, o) for o in range(groups - 1)]

    def cell_copy(o):
        return pltpu.make_async_remote_copy(
            src_ref=outgoing.at[others[o]], dst_ref=arrived.at[g],
            send_sem=cell_send.at[o], recv_sem=cell_recv.at[g],
            device_id=(others[o], d), device_id_type=MESH,
        )

    def tail_copy(o):
        other = lax.rem(g + o, groups)
        return pltpu.make_async_remote_copy(
            src_ref=tail_out.at[other], dst_ref=tail_in.at[g],
            send_sem=tail_send.at[o], recv_sem=tail_recv.at[g],
            device_id=(other, lax.rem(d + 1, columns)), device_id_type=MESH,
        )

    for o in range(groups - 1):
        build(others[o])
        cell_copy(o).start()
    build(g)
    arrived[g] = outgoing[g]

    @pl.when(d == first)
    def _():
        for o in range(groups):
            tail_copy(o).start()

    for i in range(3):
        stack_ref[i * rank:(i + 1) * rank, :] = rhs[0:rank, :]
    for i, start in enumerate(STARTS):
        weights_ref[i] = pool_weights(start)
    for t in range(tiles):
        bare = raw_ref[t].astype(jnp.float32) - dark_ref[...].astype(jnp.float32)
        own_ref[t] = jnp.where(wide < counts_ref[t], bare, 0.0)

    @pl.when(first + PAIR < columns)
    def _():
        pl.semaphore_wait(above, (columns - first - PAIR) * groups)

    @pl.loop(first + PAIR, columns)
    def _(column):
        for a in range(groups):
            stat_copy(jnp.int32(a), column).start()

    @pl.when((d > first) & (d < columns - 1))
    def _():
        for o in range(groups):
            tail_copy(o).start()

    for o in range(groups - 1):
        pltpu.make_async_remote_copy(
            src_ref=outgoing.at[others[o]], dst_ref=arrived.at[others[o]],
            send_sem=cell_send.at[o], recv_sem=cell_recv.at[others[o]],
            device_id=(others[o], d), device_id_type=MESH,
        ).wait_recv()
    there = [
        [home(positions_ref[(s * columns + d) * tiles + t]) for t in range(tiles)]
        for s in range(groups)
    ]
    slots = [
        pick((band == g, slot) for band, slot in there[s]) for s in range(groups)
    ]
    for j in range(tiles):
        origin = pick((slots[s] == j, s) for s in range(groups))
        came_ref[j] = arrived[origin].astype(jnp.float32) - dark_ref[...].astype(jnp.float32)

    spill_ref[...] = jnp.zeros_like(spill_ref)

    @pl.when(d > 0)
    def _():
        for o in range(groups):
            source = lax.rem(g + groups - o, groups)
            pltpu.make_async_remote_copy(
                src_ref=tail_out.at[source], dst_ref=tail_in.at[source],
                send_sem=tail_send.at[o], recv_sem=tail_recv.at[source],
                device_id=(source, lax.rem(d + columns - 1, columns)), device_id_type=MESH,
            ).wait_recv()
        before = [
            [home(positions_ref[(s * columns + d - 1) * tiles + t]) for t in range(tiles)]
            for s in range(groups)
        ]
        final = pick(
            ((band == g) & (slot == tiles - 1), s)
            for s in range(groups) for band, slot in before[s]
        )
        for row in range(ROWS):
            span = slice((row + 1) * COLS - OVL, (row + 1) * COLS)
            spill_ref[row] = (
                tail_in[final, row].astype(jnp.float32) - dark_ref[:, span].astype(jnp.float32)
            )

    everything = pltpu.make_async_remote_copy(
        src_ref=inbox, dst_ref=inbox, send_sem=stat_send, recv_sem=stat_recv,
        device_id=layer[0], device_id_type=MESH,
    )
    everything.wait_recv()
    sums_ref[...] = jnp.sum(inbox[...], axis=0) + mine[...]

    everything.wait_send()
    for o in range(groups - 1):
        cell_copy(o).wait_send()

    @pl.when(d < columns - 1)
    def _():
        for o in range(groups):
            tail_copy(o).wait_send()


def finish(
    own_ref, came_ref, spill_ref, sums_ref, stack_ref, weights_ref,
    corrected_hbm, pooled_hbm, corrected_ref, pooled_ref, made_ref, inverse_ref, sems, pooled_sem,
):
    tiles, planes, pixels = own_ref.shape
    rank = stack_ref.shape[0] // 3
    chunks = sems.shape[0]
    chunk = pixels // chunks
    half_step = (COLS - OVL) // 2
    bf16, f32 = jnp.bfloat16, jnp.float32

    ratio = jnp.broadcast_to(sums_ref[0:1, :] / sums_ref[1:2, :], (planes, LANES))
    plane = lax.broadcasted_iota(jnp.int32, (planes, LANES), 0)
    lane = lax.broadcasted_iota(jnp.int32, (planes, LANES), 1)
    folded = jnp.where(lane // rank == plane, ratio, 0.0)
    shift = LANES // 2
    while shift >= rank:
        folded = folded + pltpu.roll(folded, shift, 1)
        shift //= 2
    coef = folded[:, 0:rank]
    high = coef.astype(bf16)
    rest = coef - high.astype(f32)
    middle = rest.astype(bf16)
    low = (rest - middle.astype(f32)).astype(bf16)
    parts = jnp.concatenate([low, middle, high], axis=1)

    stores = []
    for c in range(chunks):
        for block in range(c * chunk // BLOCK, (c + 1) * chunk // BLOCK):
            span = slice(block * BLOCK, (block + 1) * BLOCK)
            shade = jnp.dot(parts, stack_ref[:, span], preferred_element_type=f32)
            inverse = jnp.exp(-shade)
            inverse_ref[:, span] = inverse
            for t in range(tiles):
                corrected_ref[t, :, span] = (own_ref[t, :, span] * inverse).astype(bf16)
                made_ref[t, :, span] = (came_ref[t, :, span] * inverse).astype(bf16)
        span = slice(c * chunk, (c + 1) * chunk)
        copy = pltpu.make_async_copy(
            corrected_ref.at[:, :, span], corrected_hbm.at[:, :, span], sems.at[c]
        )
        copy.start()
        stores.append(copy)

    blocks = tiles * half_step // LANES
    pieces = [[] for _ in range(blocks + 1)]

    def pool(which, base, kind, low_row, rows):
        total = None
        for row in range(ROWS):
            at = row * COLS + base
            lhs = jnp.concatenate([made_ref[j, :, at:at + rows] for j in which], axis=0)
            part = jnp.dot(
                lhs, weights_ref[kind, low_row:low_row + rows, :], preferred_element_type=f32
            )
            total = part if total is None else total + part
        total = total.astype(bf16).astype(f32)
        for i, j in enumerate(which):
            at = (2 * j * half_step + base - low_row) // BLOCK
            pieces[at].append(total[i * planes:(i + 1) * planes])

    even = list(range(0, tiles, 2))
    odd = list(range(1, tiles, 2))
    for base in range(0, COLS, BLOCK):
        pool(even, base, 0 if base == 0 else 2 if base == COLS - BLOCK else 1, 0, BLOCK)
    pool(odd, 0, 3, OVL, BLOCK - OVL)
    for base in range(OVL, COLS - OVL, BLOCK):
        pool(odd, base, 1, 0, BLOCK)
    pool(odd, COLS - OVL, 4, 0, OVL)

    spill = None
    for row in range(ROWS):
        span = slice((row + 1) * COLS - OVL, (row + 1) * COLS)
        fixed = (spill_ref[row] * inverse_ref[:, span]).astype(bf16)
        part = jnp.dot(fixed, weights_ref[4, 0:OVL, :], preferred_element_type=f32)
        spill = part if spill is None else spill + part
    pieces[0].append(spill.astype(bf16).astype(f32))
    for at in range(blocks):
        total = pieces[at][0]
        for piece in pieces[at][1:]:
            total = total + piece
        pooled_ref[:, at * LANES:(at + 1) * LANES] = total.astype(bf16)
    copy = pltpu.make_async_copy(pooled_ref, pooled_hbm, pooled_sem)
    copy.start()
    for done in stores + [copy]:
        done.wait()


def per_device(groups, columns, raw, dark, basis, counts, positions):
    tiles, planes, pixels = raw.shape
    rank = basis.shape[0]
    half_step = (COLS - OVL) // 2
    bf16, f32 = jnp.bfloat16, jnp.float32
    vmem = pl.BlockSpec(memory_space=pltpu.VMEM)
    anywhere = pl.BlockSpec(memory_space=pl.ANY)
    dma = pltpu.SemaphoreType.DMA
    chunks = 4
    passed = pl.pallas_call(
        functools.partial(gather, groups, columns),
        out_shape=(
            jax.ShapeDtypeStruct(raw.shape, f32),
            jax.ShapeDtypeStruct(raw.shape, f32),
            jax.ShapeDtypeStruct((ROWS, planes, OVL), f32),
            jax.ShapeDtypeStruct((2, LANES), f32),
            jax.ShapeDtypeStruct((3 * rank, pixels), bf16),
            jax.ShapeDtypeStruct((len(STARTS), BLOCK, LANES), bf16),
        ),
        in_specs=[anywhere] * 5,
        out_specs=[vmem] * 6,
        scratch_shapes=[
            pltpu.SMEM(counts.shape, jnp.int32),
            pltpu.SMEM(positions.shape, jnp.int32),
            pltpu.VMEM(raw.shape, bf16),
            pltpu.VMEM(dark.shape, bf16),
            pltpu.VMEM((16, pixels), bf16),
            pltpu.VMEM((planes, LANES), f32),
            pltpu.VMEM((2, LANES), f32),
            pltpu.VMEM((groups * columns - 1, 2, LANES), f32),
            pltpu.VMEM((groups, planes, pixels), bf16),
            pltpu.VMEM((groups, planes, pixels), bf16),
            pltpu.VMEM((groups, ROWS, planes, OVL), bf16),
            pltpu.VMEM((groups, ROWS, planes, OVL), bf16),
            dma((4,)), dma((chunks,)), pltpu.SemaphoreType.REGULAR,
            dma(()), dma(()),
            dma((groups,)), dma((groups,)), dma((groups,)), dma((groups,)),
        ],
        compiler_params=pltpu.CompilerParams(
            collective_id=0, has_side_effects=True, vmem_limit_bytes=24 << 20
        ),
    )(*[pltpu.with_memory_space_constraint(x, pltpu.HBM) for x in (counts, positions, raw, dark, basis)])
    corrected, pooled = pl.pallas_call(
        finish,
        out_shape=(
            jax.ShapeDtypeStruct(raw.shape, bf16),
            jax.ShapeDtypeStruct((planes, tiles * half_step), bf16),
        ),
        in_specs=[vmem] * 6,
        out_specs=(anywhere, anywhere),
        scratch_shapes=[
            pltpu.VMEM(raw.shape, bf16),
            pltpu.VMEM((planes, tiles * half_step), bf16),
            pltpu.VMEM(raw.shape, bf16),
            pltpu.VMEM((planes, pixels), f32),
            dma((chunks,)), dma(()),
        ],
        compiler_params=pltpu.CompilerParams(vmem_limit_bytes=24 << 20),
    )(*passed)
    return corrected, pooled.reshape(1, planes, ROWS // 2, tiles * half_step)


def solution(mesh):
    in_specs = (P(("grp", "dev"), None, None), P(), P(), P(("grp", "dev")), P())
    out_specs = (P(("grp", "dev"), None, None), P("grp", None, None, "dev"))
    return jax.shard_map(
        functools.partial(per_device, mesh.shape["grp"], mesh.shape["dev"]),
        mesh=mesh, in_specs=in_specs, out_specs=out_specs, check_vma=False,
    )
```

```python
import functools

import jax
import jax.numpy as jnp
from jax import lax
from jax.experimental import pallas as pl
from jax.experimental.pallas import tpu as pltpu
from jax.sharding import PartitionSpec as P

ROWS = 2
COLS = 2048
OVL = 128
LANES = 128
BLOCK = 256
PAIR = 2
MESH = pl.DeviceIdType.MESH
NT = (((1,), (1,)), ((), ()))


def pick(options):
    found = jnp.int32(0)
    for hit, value in options:
        found = jnp.where(hit, value, found)
    return found


def pool_weights(start):
    row = lax.broadcasted_iota(jnp.int32, (BLOCK, LANES), 0)
    lane = lax.broadcasted_iota(jnp.int32, (BLOCK, LANES), 1)
    column = (row + start).astype(jnp.float32) + 0.5
    ramp = jnp.minimum(1.0, jnp.minimum(column / OVL, (COLS - column) / OVL))
    inside = (row >= 2 * lane) & (row < 2 * lane + 2)
    return jnp.where(inside, 0.25 * jnp.maximum(ramp, 0.0), 0.0).astype(jnp.bfloat16)


STARTS = (0, BLOCK, COLS - BLOCK, -OVL, COLS - OVL)


def gather(
    groups, columns,
    counts_hbm, positions_hbm, raw_hbm, dark_hbm, basis_hbm,
    own_ref, arrived, origin_ref, spill_ref, sums_ref, stack_ref, weights_ref,
    counts_ref, positions_ref, raw_ref, dark_ref, rhs, stat, mine, inbox, outgoing, tail_out, tail_in,
    in_sem, raw_sem, above, stat_send, stat_recv, cell_send, cell_recv, tail_send, tail_recv,
):
    tiles, planes, pixels = raw_ref.shape
    rank = basis_hbm.shape[0]
    band_size = columns * tiles
    devices = groups * columns
    g = lax.axis_index("grp")
    d = lax.axis_index("dev")
    first = lax.div(d, PAIR) * PAIR
    me = d * groups + g

    loads = [
        pltpu.make_async_copy(raw_hbm, raw_ref, raw_sem),
        pltpu.make_async_copy(basis_hbm, rhs.at[0:rank], in_sem.at[0]),
        pltpu.make_async_copy(dark_hbm, dark_ref, in_sem.at[1]),
        pltpu.make_async_copy(counts_hbm, counts_ref, in_sem.at[2]),
        pltpu.make_async_copy(positions_hbm, positions_ref, in_sem.at[3]),
    ]
    for copy in loads:
        copy.start()

    barrier = pltpu.get_barrier_semaphore()
    layer = [
        (lax.rem(g + a, groups), first + lax.rem(d - first + b, PAIR))
        for b in range(PAIR) for a in range(groups) if a or b
    ]
    for where in layer:
        pl.semaphore_signal(barrier, inc=1, device_id=where, device_id_type=MESH)

    @pl.loop(first + PAIR, columns)
    def _(column):
        for a in range(groups):
            pl.semaphore_signal(
                barrier, inc=1, device_id=(jnp.int32(a), column), device_id_type=MESH
            )

    pl.semaphore_wait(barrier, (first + PAIR) * groups - 1)

    @pl.loop(0, first)
    def _(column):
        for a in range(groups):
            pl.semaphore_signal(above, inc=1, device_id=(jnp.int32(a), column), device_id_type=MESH)

    rhs[rank:, :] = jnp.ones((rhs.shape[0] - rank, pixels), jnp.bfloat16)
    width = rhs.shape[0]
    stat[...] = jnp.zeros_like(stat)
    for copy in loads:
        copy.wait()
    def home(at):
        return lax.div(at, band_size), lax.rem(at, tiles)

    depth = lax.broadcasted_iota(jnp.int32, (planes, LANES), 0)

    def live(t):
        alive = jnp.where(depth < counts_ref[t], 1.0, 0.0).astype(jnp.bfloat16)
        return jnp.concatenate([alive] * (pixels // LANES), axis=1)

    mine_home = [home(positions_ref[(g * columns + d) * tiles + t]) for t in range(tiles)]

    def build(b):
        chosen = pick((mine_home[t][0] == b, t) for t in range(tiles))
        masked = (raw_ref[chosen] - dark_ref[...]) * live(chosen)
        outgoing[b] = masked
        for row in range(ROWS):
            tail_out[b, row] = masked[:, (row + 1) * COLS - OVL:(row + 1) * COLS]

    others = [jnp.where(g <= o, o + 1, o) for o in range(groups - 1)]

    def cell_copy(o):
        return pltpu.make_async_remote_copy(
            src_ref=outgoing.at[others[o]], dst_ref=arrived.at[g],
            send_sem=cell_send.at[o], recv_sem=cell_recv.at[g],
            device_id=(others[o], d), device_id_type=MESH,
        )

    def tail_copy(o):
        other = lax.rem(g + o, groups)
        return pltpu.make_async_remote_copy(
            src_ref=tail_out.at[other], dst_ref=tail_in.at[g],
            send_sem=tail_send.at[o], recv_sem=tail_recv.at[g],
            device_id=(other, lax.rem(d + 1, columns)), device_id_type=MESH,
        )

    for o in range(groups - 1):
        build(others[o])
        cell_copy(o).start()
    build(g)
    arrived[g] = outgoing[g]

    @pl.when(d == first)
    def _():
        for o in range(groups):
            tail_copy(o).start()

    lhs = jnp.concatenate([raw_ref[...].reshape(tiles * planes, pixels), dark_ref[...]], axis=0)
    sums = lax.dot_general(lhs, rhs[...], NT, preferred_element_type=jnp.float32)
    dark_sums = sums[tiles * planes:]
    plane = lax.broadcasted_iota(jnp.int32, (planes, width), 0)
    local = jnp.zeros((planes, width), jnp.float32)
    for t in range(tiles):
        part = sums[t * planes:(t + 1) * planes] - dark_sums
        local = local + jnp.where(plane < counts_ref[t], part, 0.0)
    stat[:, 0:width] = local
    lane = lax.broadcasted_iota(jnp.int32, (planes, LANES), 1)
    for i, turned in enumerate((stat[...], pltpu.roll(stat[...], LANES - rank, 1))):
        kept = jnp.where(lane < rank, turned, 0.0)
        spread = pltpu.roll(kept, 0, 1, stride=rank, stride_axis=0)
        mine[i:i + 1, :] = jnp.sum(spread, axis=0, keepdims=True)

    def stat_copy(a, column):
        slot = lax.rem(me - (column * groups + a) + devices, devices) - 1
        return pltpu.make_async_remote_copy(
            src_ref=mine, dst_ref=inbox.at[slot], send_sem=stat_send, recv_sem=stat_recv,
            device_id=(a, column), device_id_type=MESH,
        )

    @pl.loop(0, first)
    def _(column):
        for a in range(groups):
            stat_copy(jnp.int32(a), column).start()

    for a, column in layer:
        stat_copy(a, column).start()

    for p in range(planes):
        stack_ref[p * rank:(p + 1) * rank, :] = rhs[0:rank, :]
    for i, start in enumerate(STARTS):
        weights_ref[i] = pool_weights(start)
    for t in range(tiles):
        bare = raw_ref[t].astype(jnp.float32) - dark_ref[...].astype(jnp.float32)
        own_ref[t] = bare * live(t).astype(jnp.float32)

    there = [
        [home(positions_ref[(s * columns + d) * tiles + t]) for t in range(tiles)]
        for s in range(groups)
    ]
    slots = [
        pick((band == g, slot) for band, slot in there[s]) for s in range(groups)
    ]
    for j in range(tiles):
        origin = pick((slots[s] == j, s) for s in range(groups))
        origin_ref[j:j + 1, :] = jnp.full((1, LANES), origin, jnp.int32)

    @pl.when(first + PAIR < columns)
    def _():
        pl.semaphore_wait(above, (columns - first - PAIR) * groups)

    @pl.loop(first + PAIR, columns)
    def _(column):
        for a in range(groups):
            stat_copy(jnp.int32(a), column).start()

    @pl.when((d > first) & (d < columns - 1))
    def _():
        for o in range(groups):
            tail_copy(o).start()

    spill_ref[...] = jnp.zeros_like(spill_ref)

    @pl.when(d > 0)
    def _():
        for o in range(groups):
            source = lax.rem(g + groups - o, groups)
            pltpu.make_async_remote_copy(
                src_ref=tail_out.at[source], dst_ref=tail_in.at[source],
                send_sem=tail_send.at[o], recv_sem=tail_recv.at[source],
                device_id=(source, lax.rem(d + columns - 1, columns)), device_id_type=MESH,
            ).wait_recv()
        before = [
            [home(positions_ref[(s * columns + d - 1) * tiles + t]) for t in range(tiles)]
            for s in range(groups)
        ]
        final = pick(
            ((band == g) & (slot == tiles - 1), s)
            for s in range(groups) for band, slot in before[s]
        )
        for row in range(ROWS):
            spill_ref[row] = tail_in[final, row]

    everything = pltpu.make_async_remote_copy(
        src_ref=inbox, dst_ref=inbox, send_sem=stat_send, recv_sem=stat_recv,
        device_id=layer[0], device_id_type=MESH,
    )
    for o in range(groups - 1):
        pltpu.make_async_remote_copy(
            src_ref=outgoing.at[others[o]], dst_ref=arrived.at[others[o]],
            send_sem=cell_send.at[o], recv_sem=cell_recv.at[others[o]],
            device_id=(others[o], d), device_id_type=MESH,
        ).wait_recv()
    everything.wait_recv()
    sums_ref[...] = jnp.sum(inbox[...], axis=0) + mine[...]

    everything.wait_send()
    for o in range(groups - 1):
        cell_copy(o).wait_send()

    @pl.when(d < columns - 1)
    def _():
        for o in range(groups):
            tail_copy(o).wait_send()


def finish(
    own_ref, came_ref, origin_hbm, spill_ref, sums_ref, stack_ref, weights_ref,
    corrected_hbm, pooled_hbm,
    origin_ref, corrected_ref, pooled_ref, made_ref, inverse_ref, sems, pooled_sem, origin_sem,
):
    tiles, planes, pixels = own_ref.shape
    rank = stack_ref.shape[0] // planes
    chunks = sems.shape[0]
    chunk = pixels // chunks
    half_step = (COLS - OVL) // 2
    bf16, f32 = jnp.bfloat16, jnp.float32

    find = pltpu.make_async_copy(origin_hbm, origin_ref, origin_sem)
    find.start()
    ratio = jnp.broadcast_to(sums_ref[0:1, :] / sums_ref[1:2, :], (planes, LANES))
    plane = lax.broadcasted_iota(jnp.int32, (planes, LANES), 0)
    lane = lax.broadcasted_iota(jnp.int32, (planes, LANES), 1)
    coef = jnp.where(lane // rank == plane, ratio, 0.0)
    high = coef.astype(bf16)
    rest = coef - high.astype(f32)
    middle = rest.astype(bf16)
    low = (rest - middle.astype(f32)).astype(bf16)
    parts = jnp.concatenate([low, middle, high], axis=0)

    stores = []
    for c in range(chunks):
        for block in range(c * chunk // BLOCK, (c + 1) * chunk // BLOCK):
            span = slice(block * BLOCK, (block + 1) * BLOCK)
            shades = jnp.dot(parts, stack_ref[:, span], preferred_element_type=f32)
            shade = shades[0:planes] + shades[planes:2 * planes] + shades[2 * planes:]
            inverse = jnp.exp(-shade)
            inverse_ref[:, span] = inverse
            for t in range(tiles):
                corrected_ref[t, :, span] = (own_ref[t, :, span] * inverse).astype(bf16)
                made_ref[t, :, span] = (came_ref[t, :, span].astype(f32) * inverse).astype(bf16)
        span = slice(c * chunk, (c + 1) * chunk)
        copy = pltpu.make_async_copy(
            corrected_ref.at[:, :, span], corrected_hbm.at[:, :, span], sems.at[c]
        )
        copy.start()
        stores.append(copy)

    find.wait()
    origin = [origin_ref[j, 0] for j in range(tiles)]
    blocks = tiles * half_step // LANES
    pieces = [[] for _ in range(blocks + 1)]
    even = list(range(0, tiles, 2))
    odd = list(range(1, tiles, 2))

    def pool(kind, low_row, rows, windows):
        parts = []
        for row in range(ROWS):
            for which, base in windows:
                at = row * COLS + base
                parts += [made_ref[origin[j], :, at:at + rows] for j in which]
        made = jnp.dot(
            jnp.concatenate(parts, axis=0), weights_ref[kind, low_row:low_row + rows, :],
            preferred_element_type=f32,
        )
        half = made.shape[0] // ROWS
        total = made[0:half]
        for row in range(1, ROWS):
            total = total + made[row * half:(row + 1) * half]
        total = total.astype(bf16).astype(f32)
        i = 0
        for which, base in windows:
            for j in which:
                at = (2 * j * half_step + base - low_row) // BLOCK
                pieces[at].append(total[i * planes:(i + 1) * planes])
                i += 1

    pool(0, 0, BLOCK, [(even, 0)])
    pool(2, 0, BLOCK, [(even, COLS - BLOCK)])
    pool(3, OVL, BLOCK - OVL, [(odd, 0)])
    pool(4, 0, OVL, [(odd, COLS - OVL)])
    pool(1, 0, BLOCK, [(even, base) for base in range(BLOCK, COLS - BLOCK, BLOCK)]
         + [(odd, base) for base in range(OVL, COLS - OVL, BLOCK)])

    spill = None
    for row in range(ROWS):
        span = slice((row + 1) * COLS - OVL, (row + 1) * COLS)
        fixed = (spill_ref[row].astype(f32) * inverse_ref[:, span]).astype(bf16)
        part = jnp.dot(fixed, weights_ref[4, 0:OVL, :], preferred_element_type=f32)
        spill = part if spill is None else spill + part
    pieces[0].append(spill.astype(bf16).astype(f32))
    for at in range(blocks):
        total = pieces[at][0]
        for piece in pieces[at][1:]:
            total = total + piece
        pooled_ref[:, at * LANES:(at + 1) * LANES] = total.astype(bf16)
    copy = pltpu.make_async_copy(pooled_ref, pooled_hbm, pooled_sem)
    copy.start()
    for done in stores + [copy]:
        done.wait()


def per_device(groups, columns, raw, dark, basis, counts, positions):
    tiles, planes, pixels = raw.shape
    rank = basis.shape[0]
    half_step = (COLS - OVL) // 2
    bf16, f32 = jnp.bfloat16, jnp.float32
    vmem = pl.BlockSpec(memory_space=pltpu.VMEM)
    anywhere = pl.BlockSpec(memory_space=pl.ANY)
    dma = pltpu.SemaphoreType.DMA
    chunks = 2
    passed = pl.pallas_call(
        functools.partial(gather, groups, columns),
        out_shape=(
            jax.ShapeDtypeStruct(raw.shape, f32),
            jax.ShapeDtypeStruct((groups, planes, pixels), bf16),
            jax.ShapeDtypeStruct((tiles, LANES), jnp.int32),
            jax.ShapeDtypeStruct((ROWS, planes, OVL), bf16),
            jax.ShapeDtypeStruct((2, LANES), f32),
            jax.ShapeDtypeStruct((planes * rank, pixels), bf16),
            jax.ShapeDtypeStruct((len(STARTS), BLOCK, LANES), bf16),
        ),
        in_specs=[anywhere] * 5,
        out_specs=[vmem] * 7,
        scratch_shapes=[
            pltpu.SMEM(counts.shape, jnp.int32),
            pltpu.SMEM(positions.shape, jnp.int32),
            pltpu.VMEM(raw.shape, bf16),
            pltpu.VMEM(dark.shape, bf16),
            pltpu.VMEM((16, pixels), bf16),
            pltpu.VMEM((planes, LANES), f32),
            pltpu.VMEM((2, LANES), f32),
            pltpu.VMEM((groups * columns - 1, 2, LANES), f32),
            pltpu.VMEM((groups, planes, pixels), bf16),
            pltpu.VMEM((groups, ROWS, planes, OVL), bf16),
            pltpu.VMEM((groups, ROWS, planes, OVL), bf16),
            dma((4,)), dma(()), pltpu.SemaphoreType.REGULAR,
            dma(()), dma(()),
            dma((groups,)), dma((groups,)), dma((groups,)), dma((groups,)),
        ],
        compiler_params=pltpu.CompilerParams(
            collective_id=0, has_side_effects=True, vmem_limit_bytes=24 << 20
        ),
    )(*[pltpu.with_memory_space_constraint(x, pltpu.HBM) for x in (counts, positions, raw, dark, basis)])
    corrected, pooled = pl.pallas_call(
        finish,
        out_shape=(
            jax.ShapeDtypeStruct(raw.shape, bf16),
            jax.ShapeDtypeStruct((planes, tiles * half_step), bf16),
        ),
        in_specs=[vmem] * 7,
        out_specs=(anywhere, anywhere),
        scratch_shapes=[
            pltpu.SMEM((tiles, LANES), jnp.int32),
            pltpu.VMEM(raw.shape, bf16),
            pltpu.VMEM((planes, tiles * half_step), bf16),
            pltpu.VMEM(raw.shape, bf16),
            pltpu.VMEM((planes, pixels), f32),
            dma((chunks,)), dma(()), dma(()),
        ],
        compiler_params=pltpu.CompilerParams(vmem_limit_bytes=24 << 20),
    )(*passed)
    return corrected, pooled.reshape(1, planes, ROWS // 2, tiles * half_step)


def solution(mesh):
    in_specs = (P(("grp", "dev"), None, None), P(), P(), P(("grp", "dev")), P())
    out_specs = (P(("grp", "dev"), None, None), P("grp", None, None, "dev"))
    return jax.shard_map(
        functools.partial(per_device, mesh.shape["grp"], mesh.shape["dev"]),
        mesh=mesh, in_specs=in_specs, out_specs=out_specs, check_vma=False,
    )
```

```python
import functools

import jax
import jax.numpy as jnp
from jax import lax
from jax.experimental import pallas as pl
from jax.experimental.pallas import tpu as pltpu
from jax.sharding import PartitionSpec as P

ROWS = 2
COLS = 2048
OVL = 128
LANES = 128
BLOCK = 256
PAIR = 2
HEAD = 1024
MESH = pl.DeviceIdType.MESH
NT = (((1,), (1,)), ((), ()))


def pick(options):
    found = jnp.int32(0)
    for hit, value in options:
        found = jnp.where(hit, value, found)
    return found


def pool_weights(start):
    row = lax.broadcasted_iota(jnp.int32, (BLOCK, LANES), 0)
    lane = lax.broadcasted_iota(jnp.int32, (BLOCK, LANES), 1)
    column = (row + start).astype(jnp.float32) + 0.5
    ramp = jnp.minimum(1.0, jnp.minimum(column / OVL, (COLS - column) / OVL))
    inside = (row >= 2 * lane) & (row < 2 * lane + 2)
    return jnp.where(inside, 0.25 * jnp.maximum(ramp, 0.0), 0.0).astype(jnp.bfloat16)


STARTS = (0, BLOCK, COLS - BLOCK, -OVL, COLS - OVL)


def gather(
    groups, columns,
    counts_hbm, positions_hbm, raw_hbm, dark_hbm, basis_hbm,
    corrected_ref, made_ref, spill_ref, weights_ref,
    counts_ref, positions_ref, raw_ref, dark_ref, rhs, stat, mine, inbox, outgoing, arrived, tail_out, tail_in,
    own_ref, stack_ref, inverse_ref,
    in_sem, raw_sem, above, stat_send, stat_recv, cell_send, cell_recv, tail_send, tail_recv,
):
    tiles, planes, pixels = raw_ref.shape
    rank = basis_hbm.shape[0]
    band_size = columns * tiles
    devices = groups * columns
    g = lax.axis_index("grp")
    d = lax.axis_index("dev")
    first = lax.div(d, PAIR) * PAIR
    me = d * groups + g

    loads = [
        pltpu.make_async_copy(raw_hbm, raw_ref, raw_sem),
        pltpu.make_async_copy(basis_hbm, rhs.at[0:rank], in_sem.at[0]),
        pltpu.make_async_copy(dark_hbm, dark_ref, in_sem.at[1]),
        pltpu.make_async_copy(counts_hbm, counts_ref, in_sem.at[2]),
        pltpu.make_async_copy(positions_hbm, positions_ref, in_sem.at[3]),
    ]
    for copy in loads:
        copy.start()

    barrier = pltpu.get_barrier_semaphore()
    layer = [
        (lax.rem(g + a, groups), first + lax.rem(d - first + b, PAIR))
        for b in range(PAIR) for a in range(groups) if a or b
    ]
    for where in layer:
        pl.semaphore_signal(barrier, inc=1, device_id=where, device_id_type=MESH)

    @pl.loop(first + PAIR, columns)
    def _(column):
        for a in range(groups):
            pl.semaphore_signal(
                barrier, inc=1, device_id=(jnp.int32(a), column), device_id_type=MESH
            )

    pl.semaphore_wait(barrier, (first + PAIR) * groups - 1)

    @pl.loop(0, first)
    def _(column):
        for a in range(groups):
            pl.semaphore_signal(above, inc=1, device_id=(jnp.int32(a), column), device_id_type=MESH)

    rhs[rank:, :] = jnp.ones((rhs.shape[0] - rank, pixels), jnp.bfloat16)
    width = rhs.shape[0]
    stat[...] = jnp.zeros_like(stat)
    for copy in loads:
        copy.wait()
    def home(at):
        return lax.div(at, band_size), lax.rem(at, tiles)

    depth = lax.broadcasted_iota(jnp.int32, (planes, LANES), 0)

    def live(t):
        alive = jnp.where(depth < counts_ref[t], 1.0, 0.0).astype(jnp.bfloat16)
        return jnp.concatenate([alive] * (pixels // LANES), axis=1)

    mine_home = [home(positions_ref[(g * columns + d) * tiles + t]) for t in range(tiles)]

    def build(b):
        chosen = pick((mine_home[t][0] == b, t) for t in range(tiles))
        masked = (raw_ref[chosen] - dark_ref[...]) * live(chosen)
        outgoing[b] = masked
        for row in range(ROWS):
            tail_out[b, row] = masked[:, (row + 1) * COLS - OVL:(row + 1) * COLS]

    parts = [slice(0, HEAD), slice(HEAD, pixels)]
    others = [jnp.where(g <= o, o + 1, o) for o in range(groups - 1)]

    def cell_copy(o, part):
        return pltpu.make_async_remote_copy(
            src_ref=outgoing.at[others[o], :, parts[part]], dst_ref=arrived.at[g, :, parts[part]],
            send_sem=cell_send.at[part, o], recv_sem=cell_recv.at[part, g],
            device_id=(others[o], d), device_id_type=MESH,
        )

    def tail_copy(o):
        other = lax.rem(g + o, groups)
        return pltpu.make_async_remote_copy(
            src_ref=tail_out.at[other], dst_ref=tail_in.at[g],
            send_sem=tail_send.at[o], recv_sem=tail_recv.at[g],
            device_id=(other, lax.rem(d + 1, columns)), device_id_type=MESH,
        )

    build(others[0])
    cell_copy(0, 0).start()

    lhs = jnp.concatenate([raw_ref[...].reshape(tiles * planes, pixels), dark_ref[...]], axis=0)
    sums = lax.dot_general(lhs, rhs[...], NT, preferred_element_type=jnp.float32)
    dark_sums = sums[tiles * planes:]
    plane = lax.broadcasted_iota(jnp.int32, (planes, width), 0)
    local = jnp.zeros((planes, width), jnp.float32)
    for t in range(tiles):
        part = sums[t * planes:(t + 1) * planes] - dark_sums
        local = local + jnp.where(plane < counts_ref[t], part, 0.0)
    stat[:, 0:width] = local
    lane = lax.broadcasted_iota(jnp.int32, (planes, LANES), 1)
    for i, turned in enumerate((stat[...], pltpu.roll(stat[...], LANES - rank, 1))):
        kept = jnp.where(lane < rank, turned, 0.0)
        spread = pltpu.roll(kept, 0, 1, stride=rank, stride_axis=0)
        mine[i:i + 1, :] = jnp.sum(spread, axis=0, keepdims=True)

    def stat_copy(a, column):
        slot = lax.rem(me - (column * groups + a) + devices, devices) - 1
        return pltpu.make_async_remote_copy(
            src_ref=mine, dst_ref=inbox.at[slot], send_sem=stat_send, recv_sem=stat_recv,
            device_id=(a, column), device_id_type=MESH,
        )

    @pl.loop(0, first)
    def _(column):
        for a in range(groups):
            stat_copy(jnp.int32(a), column).start()

    for a, column in layer:
        stat_copy(a, column).start()

    cell_copy(0, 1).start()
    for o in range(1, groups - 1):
        build(others[o])
        cell_copy(o, 0).start()
        cell_copy(o, 1).start()
    build(g)

    @pl.when(d == first)
    def _():
        for o in range(groups):
            tail_copy(o).start()

    for p in range(planes):
        stack_ref[p * rank:(p + 1) * rank, :] = rhs[0:rank, :]
    for i, start in enumerate(STARTS):
        weights_ref[i] = pool_weights(start)
    for t in range(tiles):
        bare = raw_ref[t].astype(jnp.float32) - dark_ref[...].astype(jnp.float32)
        own_ref[t] = bare * live(t).astype(jnp.float32)

    there = [
        [home(positions_ref[(s * columns + d) * tiles + t]) for t in range(tiles)]
        for s in range(groups)
    ]
    slots = [
        pick((band == g, slot) for band, slot in there[s]) for s in range(groups)
    ]

    @pl.when(first + PAIR < columns)
    def _():
        pl.semaphore_wait(above, (columns - first - PAIR) * groups)

    @pl.loop(first + PAIR, columns)
    def _(column):
        for a in range(groups):
            stat_copy(jnp.int32(a), column).start()

    @pl.when((d > first) & (d < columns - 1))
    def _():
        for o in range(groups):
            tail_copy(o).start()

    everything = pltpu.make_async_remote_copy(
        src_ref=inbox, dst_ref=inbox, send_sem=stat_send, recv_sem=stat_recv,
        device_id=layer[0], device_id_type=MESH,
    )
    everything.wait_recv()
    sums = jnp.sum(inbox[...], axis=0) + mine[...]
    ratio = jnp.broadcast_to(sums[0:1, :] / sums[1:2, :], (planes, LANES))
    plane = lax.broadcasted_iota(jnp.int32, (planes, LANES), 0)
    lane = lax.broadcasted_iota(jnp.int32, (planes, LANES), 1)
    coef = jnp.where(lane // rank == plane, ratio, 0.0)
    high = coef.astype(jnp.bfloat16)
    rest = coef - high.astype(jnp.float32)
    middle = rest.astype(jnp.bfloat16)
    low = (rest - middle.astype(jnp.float32)).astype(jnp.bfloat16)
    split = jnp.concatenate([low, middle, high], axis=0)

    for block in range(pixels // BLOCK):
        span = slice(block * BLOCK, (block + 1) * BLOCK)
        shades = jnp.dot(split, stack_ref[:, span], preferred_element_type=jnp.float32)
        shade = shades[0:planes] + shades[planes:2 * planes] + shades[2 * planes:]
        inverse = jnp.exp(-shade)
        inverse_ref[:, span] = inverse
        for t in range(tiles):
            corrected_ref[t, :, span] = (own_ref[t, :, span] * inverse).astype(jnp.bfloat16)
    arrived[g] = outgoing[g]

    spill_ref[...] = jnp.zeros_like(spill_ref)

    @pl.when(d > 0)
    def _():
        for o in range(groups):
            source = lax.rem(g + groups - o, groups)
            pltpu.make_async_remote_copy(
                src_ref=tail_out.at[source], dst_ref=tail_in.at[source],
                send_sem=tail_send.at[o], recv_sem=tail_recv.at[source],
                device_id=(source, lax.rem(d + columns - 1, columns)), device_id_type=MESH,
            ).wait_recv()
        before = [
            [home(positions_ref[(s * columns + d - 1) * tiles + t]) for t in range(tiles)]
            for s in range(groups)
        ]
        final = pick(
            ((band == g) & (slot == tiles - 1), s)
            for s in range(groups) for band, slot in before[s]
        )
        for row in range(ROWS):
            span = slice((row + 1) * COLS - OVL, (row + 1) * COLS)
            spill_ref[row] = (
                tail_in[final, row].astype(jnp.float32) * inverse_ref[:, span]
            ).astype(jnp.bfloat16)

    for o in range(groups - 1):
        for part in range(2):
            pltpu.make_async_remote_copy(
                src_ref=outgoing.at[others[o], :, parts[part]],
                dst_ref=arrived.at[others[o], :, parts[part]],
                send_sem=cell_send.at[part, o], recv_sem=cell_recv.at[part, others[o]],
                device_id=(others[o], d), device_id_type=MESH,
            ).wait_recv()
    for j in range(tiles):
        origin = pick((slots[s] == j, s) for s in range(groups))
        made_ref[j] = (arrived[origin].astype(jnp.float32) * inverse_ref[...]).astype(jnp.bfloat16)

    everything.wait_send()
    for o in range(groups - 1):
        for part in range(2):
            cell_copy(o, part).wait_send()

    @pl.when(d < columns - 1)
    def _():
        for o in range(groups):
            tail_copy(o).wait_send()


def finish(
    corrected_ref, made_ref, spill_ref, weights_ref,
    corrected_hbm, pooled_hbm,
    pooled_ref, sems, pooled_sem,
):
    tiles, planes, _ = corrected_ref.shape
    half_step = (COLS - OVL) // 2
    bf16, f32 = jnp.bfloat16, jnp.float32

    stores = [
        pltpu.make_async_copy(corrected_ref.at[t], corrected_hbm.at[t], sems.at[t])
        for t in range(tiles)
    ]
    for copy in stores:
        copy.start()
    blocks = tiles * half_step // LANES
    pieces = [[] for _ in range(blocks + 1)]
    even = list(range(0, tiles, 2))
    odd = list(range(1, tiles, 2))

    def pool(kind, low_row, rows, windows):
        parts = []
        for row in range(ROWS):
            for which, base in windows:
                at = row * COLS + base
                parts += [made_ref[j, :, at:at + rows] for j in which]
        made = jnp.dot(
            jnp.concatenate(parts, axis=0), weights_ref[kind, low_row:low_row + rows, :],
            preferred_element_type=f32,
        )
        half = made.shape[0] // ROWS
        total = made[0:half]
        for row in range(1, ROWS):
            total = total + made[row * half:(row + 1) * half]
        total = total.astype(bf16).astype(f32)
        i = 0
        for which, base in windows:
            for j in which:
                at = (2 * j * half_step + base - low_row) // BLOCK
                pieces[at].append(total[i * planes:(i + 1) * planes])
                i += 1

    pool(0, 0, BLOCK, [(even, 0)])
    pool(2, 0, BLOCK, [(even, COLS - BLOCK)])
    pool(3, OVL, BLOCK - OVL, [(odd, 0)])
    pool(4, 0, OVL, [(odd, COLS - OVL)])
    pool(1, 0, BLOCK, [(even, base) for base in range(BLOCK, COLS - BLOCK, BLOCK)]
         + [(odd, base) for base in range(OVL, COLS - OVL, BLOCK)])

    spill = None
    for row in range(ROWS):
        part = jnp.dot(spill_ref[row], weights_ref[4, 0:OVL, :], preferred_element_type=f32)
        spill = part if spill is None else spill + part
    pieces[0].append(spill.astype(bf16).astype(f32))
    for at in range(blocks):
        total = pieces[at][0]
        for piece in pieces[at][1:]:
            total = total + piece
        pooled_ref[:, at * LANES:(at + 1) * LANES] = total.astype(bf16)
    copy = pltpu.make_async_copy(pooled_ref, pooled_hbm, pooled_sem)
    copy.start()
    for done in stores + [copy]:
        done.wait()


def per_device(groups, columns, raw, dark, basis, counts, positions):
    tiles, planes, pixels = raw.shape
    rank = basis.shape[0]
    half_step = (COLS - OVL) // 2
    bf16, f32 = jnp.bfloat16, jnp.float32
    vmem = pl.BlockSpec(memory_space=pltpu.VMEM)
    anywhere = pl.BlockSpec(memory_space=pl.ANY)
    dma = pltpu.SemaphoreType.DMA
    passed = pl.pallas_call(
        functools.partial(gather, groups, columns),
        out_shape=(
            jax.ShapeDtypeStruct(raw.shape, bf16),
            jax.ShapeDtypeStruct((groups, planes, pixels), bf16),
            jax.ShapeDtypeStruct((ROWS, planes, OVL), bf16),
            jax.ShapeDtypeStruct((len(STARTS), BLOCK, LANES), bf16),
        ),
        in_specs=[anywhere] * 5,
        out_specs=[vmem] * 4,
        scratch_shapes=[
            pltpu.SMEM(counts.shape, jnp.int32),
            pltpu.SMEM(positions.shape, jnp.int32),
            pltpu.VMEM(raw.shape, bf16),
            pltpu.VMEM(dark.shape, bf16),
            pltpu.VMEM((16, pixels), bf16),
            pltpu.VMEM((planes, LANES), f32),
            pltpu.VMEM((2, LANES), f32),
            pltpu.VMEM((groups * columns - 1, 2, LANES), f32),
            pltpu.VMEM((groups, planes, pixels), bf16),
            pltpu.VMEM((groups, planes, pixels), bf16),
            pltpu.VMEM((groups, ROWS, planes, OVL), bf16),
            pltpu.VMEM((groups, ROWS, planes, OVL), bf16),
            pltpu.VMEM(raw.shape, f32),
            pltpu.VMEM((planes * rank, pixels), bf16),
            pltpu.VMEM((planes, pixels), f32),
            dma((4,)), dma(()), pltpu.SemaphoreType.REGULAR,
            dma(()), dma(()),
            dma((2, groups)), dma((2, groups)), dma((groups,)), dma((groups,)),
        ],
        compiler_params=pltpu.CompilerParams(
            collective_id=0, has_side_effects=True, vmem_limit_bytes=24 << 20
        ),
    )(*[pltpu.with_memory_space_constraint(x, pltpu.HBM) for x in (counts, positions, raw, dark, basis)])
    corrected, pooled = pl.pallas_call(
        finish,
        out_shape=(
            jax.ShapeDtypeStruct(raw.shape, bf16),
            jax.ShapeDtypeStruct((planes, tiles * half_step), bf16),
        ),
        in_specs=[vmem] * 4,
        out_specs=(anywhere, anywhere),
        scratch_shapes=[
            pltpu.VMEM((planes, tiles * half_step), bf16),
            dma((tiles,)), dma(()),
        ],
        compiler_params=pltpu.CompilerParams(vmem_limit_bytes=8 << 20),
    )(*passed)
    return corrected, pooled.reshape(1, planes, ROWS // 2, tiles * half_step)


def solution(mesh):
    in_specs = (P(("grp", "dev"), None, None), P(), P(), P(("grp", "dev")), P())
    out_specs = (P(("grp", "dev"), None, None), P("grp", None, None, "dev"))
    return jax.shard_map(
        functools.partial(per_device, mesh.shape["grp"], mesh.shape["dev"]),
        mesh=mesh, in_specs=in_specs, out_specs=out_specs, check_vma=False,
    )
```

```python
import functools

import jax
import jax.numpy as jnp
from jax import lax
from jax.experimental import pallas as pl
from jax.experimental.pallas import tpu as pltpu
from jax.sharding import PartitionSpec as P

ROWS = 2
COLS = 2048
OVL = 128
LANES = 128
BLOCK = 256
PAIR = 2
HEAD = 1024
RELAY = 1
MESH = pl.DeviceIdType.MESH
NT = (((1,), (1,)), ((), ()))


def pick(options):
    found = jnp.int32(0)
    for hit, value in options:
        found = jnp.where(hit, value, found)
    return found


def pool_weights(start):
    row = lax.broadcasted_iota(jnp.int32, (BLOCK, LANES), 0)
    lane = lax.broadcasted_iota(jnp.int32, (BLOCK, LANES), 1)
    column = (row + start).astype(jnp.float32) + 0.5
    ramp = jnp.minimum(1.0, jnp.minimum(column / OVL, (COLS - column) / OVL))
    inside = (row >= 2 * lane) & (row < 2 * lane + 2)
    return jnp.where(inside, 0.25 * jnp.maximum(ramp, 0.0), 0.0).astype(jnp.bfloat16)


STARTS = (0, BLOCK, COLS - BLOCK, -OVL, COLS - OVL)


def gather(
    groups, columns,
    counts_hbm, positions_hbm, raw_hbm, dark_hbm, basis_hbm,
    corrected_ref, made_ref, origin_ref, spill_ref, weights_ref,
    counts_ref, positions_ref, raw_ref, dark_ref, rhs, stat, mine, inbox, outgoing, arrived, passing, tail_out, tail_in,
    own_ref, stack_ref, inverse_ref,
    in_sem, raw_sem, above, stat_send, stat_recv, cell_send, cell_recv, tail_send, tail_recv,
    pass_send, pass_recv, forward_send,
):
    tiles, planes, pixels = raw_ref.shape
    rank = basis_hbm.shape[0]
    band_size = columns * tiles
    devices = groups * columns
    g = lax.axis_index("grp")
    d = lax.axis_index("dev")
    first = lax.div(d, PAIR) * PAIR
    me = d * groups + g

    parts = [slice(0, HEAD), slice(HEAD, pixels)]
    early = [
        pltpu.make_async_copy(raw_hbm, raw_ref, raw_sem),
        pltpu.make_async_copy(counts_hbm, counts_ref, in_sem.at[0]),
        pltpu.make_async_copy(positions_hbm, positions_ref, in_sem.at[1]),
        pltpu.make_async_copy(dark_hbm, dark_ref, in_sem.at[2]),
    ]
    later = [
        pltpu.make_async_copy(basis_hbm, rhs.at[0:rank], in_sem.at[3]),
    ]
    for copy in early + later:
        copy.start()

    barrier = pltpu.get_barrier_semaphore()
    layer = [
        (lax.rem(g + a, groups), first + lax.rem(d - first + b, PAIR))
        for b in range(PAIR) for a in range(groups) if a or b
    ]
    for where in layer:
        pl.semaphore_signal(barrier, inc=1, device_id=where, device_id_type=MESH)

    @pl.loop(first + PAIR, columns)
    def _(column):
        for a in range(groups):
            pl.semaphore_signal(
                barrier, inc=1, device_id=(jnp.int32(a), column), device_id_type=MESH
            )

    rhs[rank:, :] = jnp.ones((rhs.shape[0] - rank, pixels), jnp.bfloat16)
    width = rhs.shape[0]
    stat[...] = jnp.zeros_like(stat)
    for copy in early:
        copy.wait()

    def home(at):
        return lax.div(at, band_size), lax.rem(at, tiles)

    depth = lax.broadcasted_iota(jnp.int32, (planes, LANES), 0)

    def alive(t):
        return jnp.where(depth < counts_ref[t], 1.0, 0.0).astype(jnp.bfloat16)

    def live(t):
        return jnp.concatenate([alive(t)] * (pixels // LANES), axis=1)

    def live_part(t, span):
        return (raw_ref[t, :, span] - dark_ref[:, span]) * live(t)[:, span]

    mine_home = [home(positions_ref[(g * columns + d) * tiles + t]) for t in range(tiles)]

    def build(b, part):
        chosen = pick((mine_home[t][0] == b, t) for t in range(tiles))
        outgoing[b, :, parts[part]] = live_part(chosen, parts[part])

    def build_tail(b):
        chosen = pick((mine_home[t][0] == b, t) for t in range(tiles))
        for row in range(ROWS):
            span = slice((row + 1) * COLS - OVL, (row + 1) * COLS)
            tail_out[b, row] = (raw_ref[chosen, :, span] - dark_ref[:, span]) * alive(chosen)

    others = [jnp.where(g <= o, o + 1, o) for o in range(groups - 1)]

    def cell_copy(o, part):
        return pltpu.make_async_remote_copy(
            src_ref=outgoing.at[others[o], :, parts[part]], dst_ref=arrived.at[g, :, parts[part]],
            send_sem=cell_send.at[part, o], recv_sem=cell_recv.at[part, g],
            device_id=(others[o], d), device_id_type=MESH,
        )

    last = groups - 1
    detour = groups > RELAY + 2

    def pass_copy():
        return pltpu.make_async_remote_copy(
            src_ref=outgoing.at[0, :, parts[0]], dst_ref=passing,
            send_sem=pass_send, recv_sem=pass_recv,
            device_id=(jnp.int32(RELAY), d), device_id_type=MESH,
        )

    def forward_copy():
        return pltpu.make_async_remote_copy(
            src_ref=passing, dst_ref=arrived.at[last, :, parts[0]],
            send_sem=forward_send, recv_sem=cell_recv.at[0, last],
            device_id=(jnp.int32(0), d), device_id_type=MESH,
        )

    def direct(o, part):
        return ((g != last) | (first > 0)) if detour and o == 0 and part == 0 else (g >= 0)

    def tail_copy(o):
        other = lax.rem(g + o, groups)
        return pltpu.make_async_remote_copy(
            src_ref=tail_out.at[other], dst_ref=tail_in.at[g],
            send_sem=tail_send.at[o], recv_sem=tail_recv.at[g],
            device_id=(other, lax.rem(d + 1, columns)), device_id_type=MESH,
        )

    for o in range(groups - 1):
        build(others[o], 0)
    pl.semaphore_wait(barrier, (first + PAIR) * groups - 1)

    @pl.loop(0, first)
    def _(column):
        for a in range(groups):
            pl.semaphore_signal(above, inc=1, device_id=(jnp.int32(a), column), device_id_type=MESH)

    if detour:
        @pl.when((g == last) & (first == 0))
        def _():
            pass_copy().start()

    for o in range(groups - 1):
        @pl.when(direct(o, 0))
        def _():
            cell_copy(o, 0).start()

    for copy in later:
        copy.wait()

    lhs = jnp.concatenate([raw_ref[...].reshape(tiles * planes, pixels), dark_ref[...]], axis=0)
    sums = lax.dot_general(lhs, rhs[...], NT, preferred_element_type=jnp.float32)
    dark_sums = sums[tiles * planes:]
    plane = lax.broadcasted_iota(jnp.int32, (planes, width), 0)
    local = jnp.zeros((planes, width), jnp.float32)
    for t in range(tiles):
        part = sums[t * planes:(t + 1) * planes] - dark_sums
        local = local + jnp.where(plane < counts_ref[t], part, 0.0)
    stat[:, 0:width] = local
    lane = lax.broadcasted_iota(jnp.int32, (planes, LANES), 1)
    for i, turned in enumerate((stat[...], pltpu.roll(stat[...], LANES - rank, 1))):
        kept = jnp.where(lane < rank, turned, 0.0)
        spread = pltpu.roll(kept, 0, 1, stride=rank, stride_axis=0)
        mine[i:i + 1, :] = jnp.sum(spread, axis=0, keepdims=True)

    def stat_copy(a, column):
        slot = lax.rem(me - (column * groups + a) + devices, devices) - 1
        return pltpu.make_async_remote_copy(
            src_ref=mine, dst_ref=inbox.at[slot], send_sem=stat_send, recv_sem=stat_recv,
            device_id=(a, column), device_id_type=MESH,
        )

    @pl.loop(0, first)
    def _(column):
        for a in range(groups):
            stat_copy(jnp.int32(a), column).start()

    for a, column in layer:
        stat_copy(a, column).start()

    for b in range(groups):
        build_tail(b)

    @pl.when(d == first)
    def _():
        for o in range(groups):
            tail_copy(o).start()

    for o in [0] + list(range(groups - 2, 0, -1)):
        build(others[o], 1)
        if detour and o == 1:
            @pl.when((g != RELAY) | (first > 0))
            def _():
                cell_copy(1, 1).start()
        else:
            cell_copy(o, 1).start()
    for part in range(2):
        build(g, part)

    for p in range(planes):
        stack_ref[p * rank:(p + 1) * rank, :] = rhs[0:rank, :]
    for i, start in enumerate(STARTS):
        weights_ref[i] = pool_weights(start)
    for t in range(tiles):
        bare = raw_ref[t].astype(jnp.float32) - dark_ref[...].astype(jnp.float32)
        own_ref[t] = bare * live(t).astype(jnp.float32)

    if detour:
        @pl.when((g == RELAY) & (first == 0))
        def _():
            pass_copy().wait_recv()
            forward_copy().start()
            cell_copy(1, 1).start()

    there = [
        [home(positions_ref[(s * columns + d) * tiles + t]) for t in range(tiles)]
        for s in range(groups)
    ]
    slots = [
        pick((band == g, slot) for band, slot in there[s]) for s in range(groups)
    ]

    @pl.when(first + PAIR < columns)
    def _():
        pl.semaphore_wait(above, (columns - first - PAIR) * groups)

    @pl.loop(first + PAIR, columns)
    def _(column):
        for a in range(groups):
            stat_copy(jnp.int32(a), column).start()

    @pl.when((d > first) & (d < columns - 1))
    def _():
        for o in range(groups):
            tail_copy(o).start()

    everything = pltpu.make_async_remote_copy(
        src_ref=inbox, dst_ref=inbox, send_sem=stat_send, recv_sem=stat_recv,
        device_id=layer[0], device_id_type=MESH,
    )
    everything.wait_recv()
    sums = jnp.sum(inbox[...], axis=0) + mine[...]
    ratio = jnp.broadcast_to(sums[0:1, :] / sums[1:2, :], (planes, LANES))
    plane = lax.broadcasted_iota(jnp.int32, (planes, LANES), 0)
    lane = lax.broadcasted_iota(jnp.int32, (planes, LANES), 1)
    coef = jnp.where(lane // rank == plane, ratio, 0.0)
    high = coef.astype(jnp.bfloat16)
    rest = coef - high.astype(jnp.float32)
    middle = rest.astype(jnp.bfloat16)
    low = (rest - middle.astype(jnp.float32)).astype(jnp.bfloat16)
    split = jnp.concatenate([low, middle, high], axis=0)

    for block in range(pixels // BLOCK):
        span = slice(block * BLOCK, (block + 1) * BLOCK)
        shades = jnp.dot(split, stack_ref[:, span], preferred_element_type=jnp.float32)
        shade = shades[0:planes] + shades[planes:2 * planes] + shades[2 * planes:]
        inverse = jnp.exp(-shade)
        inverse_ref[:, span] = inverse
        for t in range(tiles):
            corrected_ref[t, :, span] = (own_ref[t, :, span] * inverse).astype(jnp.bfloat16)
    made_ref[g] = (outgoing[g].astype(jnp.float32) * inverse_ref[...]).astype(jnp.bfloat16)
    for j in range(tiles):
        origin = pick((slots[s] == j, s) for s in range(groups))
        origin_ref[j:j + 1, :] = jnp.full((1, LANES), origin, jnp.int32)

    spill_ref[...] = jnp.zeros_like(spill_ref)

    @pl.when(d > 0)
    def _():
        for o in range(groups):
            source = lax.rem(g + groups - o, groups)
            pltpu.make_async_remote_copy(
                src_ref=tail_out.at[source], dst_ref=tail_in.at[source],
                send_sem=tail_send.at[o], recv_sem=tail_recv.at[source],
                device_id=(source, lax.rem(d + columns - 1, columns)), device_id_type=MESH,
            ).wait_recv()
        before = [
            [home(positions_ref[(s * columns + d - 1) * tiles + t]) for t in range(tiles)]
            for s in range(groups)
        ]
        final = pick(
            ((band == g) & (slot == tiles - 1), s)
            for s in range(groups) for band, slot in before[s]
        )
        for row in range(ROWS):
            span = slice((row + 1) * COLS - OVL, (row + 1) * COLS)
            spill_ref[row] = (
                tail_in[final, row].astype(jnp.float32) * inverse_ref[:, span]
            ).astype(jnp.bfloat16)

    for o in range(groups - 1):
        for part in range(2):
            pltpu.make_async_remote_copy(
                src_ref=outgoing.at[others[o], :, parts[part]],
                dst_ref=arrived.at[others[o], :, parts[part]],
                send_sem=cell_send.at[part, o], recv_sem=cell_recv.at[part, others[o]],
                device_id=(others[o], d), device_id_type=MESH,
            ).wait_recv()
        made_ref[others[o]] = (
            arrived[others[o]].astype(jnp.float32) * inverse_ref[...]
        ).astype(jnp.bfloat16)

    everything.wait_send()
    for o in range(groups - 1):
        for part in range(2):
            @pl.when(direct(o, part))
            def _():
                cell_copy(o, part).wait_send()

    if detour:
        @pl.when((g == last) & (first == 0))
        def _():
            pass_copy().wait_send()

        @pl.when((g == RELAY) & (first == 0))
        def _():
            forward_copy().wait_send()

    @pl.when(d < columns - 1)
    def _():
        for o in range(groups):
            tail_copy(o).wait_send()


def finish(
    corrected_ref, made_ref, origin_ref, spill_ref, weights_ref,
    corrected_hbm, pooled_hbm,
    pooled_ref, sems, pooled_sem,
):
    tiles, planes, _ = corrected_ref.shape
    half_step = (COLS - OVL) // 2
    bf16, f32 = jnp.bfloat16, jnp.float32

    stores = [
        pltpu.make_async_copy(corrected_ref.at[t], corrected_hbm.at[t], sems.at[t])
        for t in range(tiles)
    ]
    for copy in stores:
        copy.start()
    where = origin_ref[...]
    origin = [where[j, 0] for j in range(tiles)]
    blocks = tiles * half_step // LANES
    pieces = [[] for _ in range(blocks + 1)]
    even = list(range(0, tiles, 2))
    odd = list(range(1, tiles, 2))

    def pool(kind, low_row, rows, windows):
        parts = []
        for row in range(ROWS):
            for which, base in windows:
                at = row * COLS + base
                parts += [made_ref[origin[j], :, at:at + rows] for j in which]
        made = jnp.dot(
            jnp.concatenate(parts, axis=0), weights_ref[kind, low_row:low_row + rows, :],
            preferred_element_type=f32,
        )
        half = made.shape[0] // ROWS
        total = made[0:half]
        for row in range(1, ROWS):
            total = total + made[row * half:(row + 1) * half]
        total = total.astype(bf16).astype(f32)
        i = 0
        for which, base in windows:
            for j in which:
                at = (2 * j * half_step + base - low_row) // BLOCK
                pieces[at].append(total[i * planes:(i + 1) * planes])
                i += 1

    pool(0, 0, BLOCK, [(even, 0)])
    pool(2, 0, BLOCK, [(even, COLS - BLOCK)])
    pool(3, OVL, BLOCK - OVL, [(odd, 0)])
    pool(4, 0, OVL, [(odd, COLS - OVL)])
    pool(1, 0, BLOCK, [(even, base) for base in range(BLOCK, COLS - BLOCK, BLOCK)]
         + [(odd, base) for base in range(OVL, COLS - OVL, BLOCK)])

    spill = None
    for row in range(ROWS):
        part = jnp.dot(spill_ref[row], weights_ref[4, 0:OVL, :], preferred_element_type=f32)
        spill = part if spill is None else spill + part
    pieces[0].append(spill.astype(bf16).astype(f32))
    for at in range(blocks):
        total = pieces[at][0]
        for piece in pieces[at][1:]:
            total = total + piece
        pooled_ref[:, at * LANES:(at + 1) * LANES] = total.astype(bf16)
    copy = pltpu.make_async_copy(pooled_ref, pooled_hbm, pooled_sem)
    copy.start()
    for done in stores + [copy]:
        done.wait()


def per_device(groups, columns, raw, dark, basis, counts, positions):
    tiles, planes, pixels = raw.shape
    rank = basis.shape[0]
    half_step = (COLS - OVL) // 2
    bf16, f32 = jnp.bfloat16, jnp.float32
    vmem = pl.BlockSpec(memory_space=pltpu.VMEM)
    anywhere = pl.BlockSpec(memory_space=pl.ANY)
    dma = pltpu.SemaphoreType.DMA
    passed = pl.pallas_call(
        functools.partial(gather, groups, columns),
        out_shape=(
            jax.ShapeDtypeStruct(raw.shape, bf16),
            jax.ShapeDtypeStruct((groups, planes, pixels), bf16),
            jax.ShapeDtypeStruct((tiles, LANES), jnp.int32),
            jax.ShapeDtypeStruct((ROWS, planes, OVL), bf16),
            jax.ShapeDtypeStruct((len(STARTS), BLOCK, LANES), bf16),
        ),
        in_specs=[anywhere] * 5,
        out_specs=[vmem] * 5,
        scratch_shapes=[
            pltpu.SMEM(counts.shape, jnp.int32),
            pltpu.SMEM(positions.shape, jnp.int32),
            pltpu.VMEM(raw.shape, bf16),
            pltpu.VMEM(dark.shape, bf16),
            pltpu.VMEM((16, pixels), bf16),
            pltpu.VMEM((planes, LANES), f32),
            pltpu.VMEM((2, LANES), f32),
            pltpu.VMEM((groups * columns - 1, 2, LANES), f32),
            pltpu.VMEM((groups, planes, pixels), bf16),
            pltpu.VMEM((groups, planes, pixels), bf16),
            pltpu.VMEM((planes, HEAD), bf16),
            pltpu.VMEM((groups, ROWS, planes, OVL), bf16),
            pltpu.VMEM((groups, ROWS, planes, OVL), bf16),
            pltpu.VMEM(raw.shape, f32),
            pltpu.VMEM((planes * rank, pixels), bf16),
            pltpu.VMEM((planes, pixels), f32),
            dma((4,)), dma(()), pltpu.SemaphoreType.REGULAR,
            dma(()), dma(()),
            dma((2, groups)), dma((2, groups)), dma((groups,)), dma((groups,)),
            dma(()), dma(()), dma(()),
        ],
        compiler_params=pltpu.CompilerParams(
            collective_id=0, has_side_effects=True, vmem_limit_bytes=24 << 20
        ),
    )(*[pltpu.with_memory_space_constraint(x, pltpu.HBM) for x in (counts, positions, raw, dark, basis)])
    corrected, pooled = pl.pallas_call(
        finish,
        out_shape=(
            jax.ShapeDtypeStruct(raw.shape, bf16),
            jax.ShapeDtypeStruct((planes, tiles * half_step), bf16),
        ),
        in_specs=[vmem] * 5,
        out_specs=(anywhere, anywhere),
        scratch_shapes=[
            pltpu.VMEM((planes, tiles * half_step), bf16),
            dma((tiles,)), dma(()),
        ],
        compiler_params=pltpu.CompilerParams(vmem_limit_bytes=8 << 20),
    )(*passed)
    return corrected, pooled.reshape(1, planes, ROWS // 2, tiles * half_step)


def solution(mesh):
    in_specs = (P(("grp", "dev"), None, None), P(), P(), P(("grp", "dev")), P())
    out_specs = (P(("grp", "dev"), None, None), P("grp", None, None, "dev"))
    return jax.shard_map(
        functools.partial(per_device, mesh.shape["grp"], mesh.shape["dev"]),
        mesh=mesh, in_specs=in_specs, out_specs=out_specs, check_vma=False,
    )
```

```python
import functools

import jax
import jax.numpy as jnp
from jax import lax
from jax.experimental import pallas as pl
from jax.experimental.pallas import tpu as pltpu
from jax.sharding import PartitionSpec as P

ROWS = 2
COLS = 2048
OVL = 128
LANES = 128
BLOCK = 256
PAIR = 2
HEAD = 1024
RELAY = 1
MESH = pl.DeviceIdType.MESH
NT = (((1,), (1,)), ((), ()))


def pick(options):
    found = jnp.int32(0)
    for hit, value in options:
        found = jnp.where(hit, value, found)
    return found


def pool_weights(start):
    row = lax.broadcasted_iota(jnp.int32, (BLOCK, LANES), 0)
    lane = lax.broadcasted_iota(jnp.int32, (BLOCK, LANES), 1)
    column = (row + start).astype(jnp.float32) + 0.5
    ramp = jnp.minimum(1.0, jnp.minimum(column / OVL, (COLS - column) / OVL))
    inside = (row >= 2 * lane) & (row < 2 * lane + 2)
    return jnp.where(inside, 0.25 * jnp.maximum(ramp, 0.0), 0.0).astype(jnp.bfloat16)


WINDOWS = (
    (0, 0, BLOCK), (BLOCK, 0, BLOCK), (COLS - BLOCK, 0, BLOCK),
    (-OVL, OVL, BLOCK - OVL), (COLS - OVL, 0, OVL),
)


def gather(
    groups, columns,
    counts_hbm, positions_hbm, raw_hbm, dark_hbm, basis_hbm,
    corrected_ref, made_ref, origin_ref, spill_ref, weights_ref,
    counts_ref, positions_ref, raw_head, raw_rest, dark_ref, rhs, stat, mine, inbox, outgoing, arrived, passing, tail_out, tail_in,
    own_ref, stack_ref, inverse_ref,
    in_sem, raw_sem, above, stat_send, stat_recv, cell_send, cell_recv, tail_send, tail_recv,
    pass_send, pass_recv, forward_send,
):
    tiles, planes, pixels = raw_hbm.shape
    rank = basis_hbm.shape[0]
    band_size = columns * tiles
    devices = groups * columns
    g = lax.axis_index("grp")
    d = lax.axis_index("dev")
    first = lax.div(d, PAIR) * PAIR
    me = d * groups + g

    parts = [slice(0, HEAD), slice(HEAD, pixels)]
    early = [
        pltpu.make_async_copy(raw_hbm.at[:, :, parts[0]], raw_head, raw_sem.at[0]),
        pltpu.make_async_copy(counts_hbm, counts_ref, in_sem.at[0]),
        pltpu.make_async_copy(positions_hbm, positions_ref, in_sem.at[1]),
        pltpu.make_async_copy(dark_hbm, dark_ref, in_sem.at[2]),
    ]
    later = [
        pltpu.make_async_copy(basis_hbm, rhs.at[0:rank], in_sem.at[3]),
        pltpu.make_async_copy(raw_hbm.at[:, :, parts[1]], raw_rest, raw_sem.at[1]),
    ]
    for copy in early + later:
        copy.start()

    barrier = pltpu.get_barrier_semaphore()
    layer = [
        (lax.rem(g + a, groups), first + lax.rem(d - first + b, PAIR))
        for b in range(PAIR) for a in range(groups) if a or b
    ]
    for where in layer:
        pl.semaphore_signal(barrier, inc=1, device_id=where, device_id_type=MESH)

    @pl.loop(first + PAIR, columns)
    def _(column):
        for a in range(groups):
            pl.semaphore_signal(
                barrier, inc=1, device_id=(jnp.int32(a), column), device_id_type=MESH
            )

    rhs[rank:, :] = jnp.ones((rhs.shape[0] - rank, pixels), jnp.bfloat16)
    width = rhs.shape[0]
    stat[...] = jnp.zeros_like(stat)
    for copy in early:
        copy.wait()

    def home(at):
        return lax.div(at, band_size), lax.rem(at, tiles)

    depth = lax.broadcasted_iota(jnp.int32, (planes, LANES), 0)

    def alive(t):
        return jnp.where(depth < counts_ref[t], 1.0, 0.0).astype(jnp.bfloat16)

    def live(t):
        return jnp.concatenate([alive(t)] * (pixels // LANES), axis=1)

    def live_part(t, part):
        raw = (raw_head, raw_rest)[part][t]
        return (raw - dark_ref[:, parts[part]]) * live(t)[:, parts[part]]

    mine_home = [home(positions_ref[(g * columns + d) * tiles + t]) for t in range(tiles)]

    def build(b, part):
        chosen = pick((mine_home[t][0] == b, t) for t in range(tiles))
        outgoing[b, :, parts[part]] = live_part(chosen, part)

    def build_tail(b):
        chosen = pick((mine_home[t][0] == b, t) for t in range(tiles))
        for row in range(ROWS):
            span = slice((row + 1) * COLS - OVL, (row + 1) * COLS)
            raw = raw_rest[chosen, :, span.start - HEAD:span.stop - HEAD]
            tail_out[b, row] = (raw - dark_ref[:, span]) * alive(chosen)

    others = [jnp.where(g <= o, o + 1, o) for o in range(groups - 1)]

    def cell_copy(o, part):
        return pltpu.make_async_remote_copy(
            src_ref=outgoing.at[others[o], :, parts[part]], dst_ref=arrived.at[g, :, parts[part]],
            send_sem=cell_send.at[part, o], recv_sem=cell_recv.at[part, g],
            device_id=(others[o], d), device_id_type=MESH,
        )

    last = groups - 1
    detour = groups > RELAY + 2

    def pass_copy():
        return pltpu.make_async_remote_copy(
            src_ref=outgoing.at[0, :, parts[0]], dst_ref=passing,
            send_sem=pass_send, recv_sem=pass_recv,
            device_id=(jnp.int32(RELAY), d), device_id_type=MESH,
        )

    def forward_copy():
        return pltpu.make_async_remote_copy(
            src_ref=passing, dst_ref=arrived.at[last, :, parts[0]],
            send_sem=forward_send, recv_sem=cell_recv.at[0, last],
            device_id=(jnp.int32(0), d), device_id_type=MESH,
        )

    def direct(o, part):
        return ((g != last) | (first > 0)) if detour and o == 0 and part == 0 else (g >= 0)

    def tail_copy(o):
        other = lax.rem(g + o, groups)
        return pltpu.make_async_remote_copy(
            src_ref=tail_out.at[other], dst_ref=tail_in.at[g],
            send_sem=tail_send.at[o], recv_sem=tail_recv.at[g],
            device_id=(other, lax.rem(d + 1, columns)), device_id_type=MESH,
        )

    for o in range(groups - 1):
        build(others[o], 0)
    pl.semaphore_wait(barrier, (first + PAIR) * groups - 1)

    @pl.loop(0, first)
    def _(column):
        for a in range(groups):
            pl.semaphore_signal(above, inc=1, device_id=(jnp.int32(a), column), device_id_type=MESH)

    if detour:
        @pl.when((g == last) & (first == 0))
        def _():
            pass_copy().start()

    for o in range(groups - 1):
        @pl.when(direct(o, 0))
        def _():
            cell_copy(o, 0).start()

    for copy in later:
        copy.wait()

    raw = jnp.concatenate([raw_head[...], raw_rest[...]], axis=2)
    lhs = jnp.concatenate([raw.reshape(tiles * planes, pixels), dark_ref[...]], axis=0)
    sums = lax.dot_general(lhs, rhs[...], NT, preferred_element_type=jnp.float32)
    dark_sums = sums[tiles * planes:]
    plane = lax.broadcasted_iota(jnp.int32, (planes, width), 0)
    local = jnp.zeros((planes, width), jnp.float32)
    for t in range(tiles):
        part = sums[t * planes:(t + 1) * planes] - dark_sums
        local = local + jnp.where(plane < counts_ref[t], part, 0.0)
    stat[:, 0:width] = local
    lane = lax.broadcasted_iota(jnp.int32, (planes, LANES), 1)
    for i, turned in enumerate((stat[...], pltpu.roll(stat[...], LANES - rank, 1))):
        kept = jnp.where(lane < rank, turned, 0.0)
        spread = pltpu.roll(kept, 0, 1, stride=rank, stride_axis=0)
        mine[i:i + 1, :] = jnp.sum(spread, axis=0, keepdims=True)

    def stat_copy(a, column):
        slot = lax.rem(me - (column * groups + a) + devices, devices) - 1
        return pltpu.make_async_remote_copy(
            src_ref=mine, dst_ref=inbox.at[slot], send_sem=stat_send, recv_sem=stat_recv,
            device_id=(a, column), device_id_type=MESH,
        )

    @pl.loop(0, first)
    def _(column):
        for a in range(groups):
            stat_copy(jnp.int32(a), column).start()

    for a, column in layer:
        stat_copy(a, column).start()

    for b in range(groups):
        build_tail(b)

    build(others[0], 1)
    cell_copy(0, 1).start()

    @pl.when(d == first)
    def _():
        for o in range(groups):
            tail_copy(o).start()

    for o in range(groups - 2, 0, -1):
        build(others[o], 1)
        if detour and o == 1:
            @pl.when((g != RELAY) | (first > 0))
            def _():
                cell_copy(1, 1).start()
        else:
            cell_copy(o, 1).start()
    for part in range(2):
        build(g, part)

    for p in range(planes):
        stack_ref[p * rank:(p + 1) * rank, :] = rhs[0:rank, :]
    for i, (start, low, rows) in enumerate(WINDOWS):
        for row in range(ROWS):
            weights_ref[i, row * rows:(row + 1) * rows, :] = pool_weights(start)[low:low + rows]
    for t in range(tiles):
        bare = raw[t].astype(jnp.float32) - dark_ref[...].astype(jnp.float32)
        own_ref[t] = bare * live(t).astype(jnp.float32)

    if detour:
        @pl.when((g == RELAY) & (first == 0))
        def _():
            pass_copy().wait_recv()
            forward_copy().start()
            cell_copy(1, 1).start()

    there = [
        [home(positions_ref[(s * columns + d) * tiles + t]) for t in range(tiles)]
        for s in range(groups)
    ]
    slots = [
        pick((band == g, slot) for band, slot in there[s]) for s in range(groups)
    ]

    @pl.when(first + PAIR < columns)
    def _():
        pl.semaphore_wait(above, (columns - first - PAIR) * groups)

    @pl.loop(first + PAIR, columns)
    def _(column):
        for a in range(groups):
            stat_copy(jnp.int32(a), column).start()

    @pl.when((d > first) & (d < columns - 1))
    def _():
        for o in range(groups):
            tail_copy(o).start()

    everything = pltpu.make_async_remote_copy(
        src_ref=inbox, dst_ref=inbox, send_sem=stat_send, recv_sem=stat_recv,
        device_id=layer[0], device_id_type=MESH,
    )
    everything.wait_recv()
    sums = jnp.sum(inbox[...], axis=0) + mine[...]
    ratio = jnp.broadcast_to(sums[0:1, :] / sums[1:2, :], (planes, LANES))
    plane = lax.broadcasted_iota(jnp.int32, (planes, LANES), 0)
    lane = lax.broadcasted_iota(jnp.int32, (planes, LANES), 1)
    coef = jnp.where(lane // rank == plane, ratio, 0.0)
    high = coef.astype(jnp.bfloat16)
    rest = coef - high.astype(jnp.float32)
    middle = rest.astype(jnp.bfloat16)
    low = (rest - middle.astype(jnp.float32)).astype(jnp.bfloat16)
    split = jnp.concatenate([low, middle, high], axis=0)

    for block in range(pixels // BLOCK):
        span = slice(block * BLOCK, (block + 1) * BLOCK)
        shades = jnp.dot(split, stack_ref[:, span], preferred_element_type=jnp.float32)
        shade = shades[0:planes] + shades[planes:2 * planes] + shades[2 * planes:]
        inverse = jnp.exp(-shade)
        inverse_ref[:, span] = inverse
        for t in range(tiles):
            corrected_ref[t, :, span] = (own_ref[t, :, span] * inverse).astype(jnp.bfloat16)
    made_ref[g] = (outgoing[g].astype(jnp.float32) * inverse_ref[...]).astype(jnp.bfloat16)
    for j in range(tiles):
        origin = pick((slots[s] == j, s) for s in range(groups))
        origin_ref[j:j + 1, :] = jnp.full((1, LANES), origin, jnp.int32)

    spill_ref[...] = jnp.zeros_like(spill_ref)

    @pl.when(d > 0)
    def _():
        for o in range(groups):
            source = lax.rem(g + groups - o, groups)
            pltpu.make_async_remote_copy(
                src_ref=tail_out.at[source], dst_ref=tail_in.at[source],
                send_sem=tail_send.at[o], recv_sem=tail_recv.at[source],
                device_id=(source, lax.rem(d + columns - 1, columns)), device_id_type=MESH,
            ).wait_recv()
        before = [
            [home(positions_ref[(s * columns + d - 1) * tiles + t]) for t in range(tiles)]
            for s in range(groups)
        ]
        final = pick(
            ((band == g) & (slot == tiles - 1), s)
            for s in range(groups) for band, slot in before[s]
        )
        for row in range(ROWS):
            span = slice((row + 1) * COLS - OVL, (row + 1) * COLS)
            spill_ref[row] = (
                tail_in[final, row].astype(jnp.float32) * inverse_ref[:, span]
            ).astype(jnp.bfloat16)

    for o in range(groups - 1):
        for part in range(2):
            pltpu.make_async_remote_copy(
                src_ref=outgoing.at[others[o], :, parts[part]],
                dst_ref=arrived.at[others[o], :, parts[part]],
                send_sem=cell_send.at[part, o], recv_sem=cell_recv.at[part, others[o]],
                device_id=(others[o], d), device_id_type=MESH,
            ).wait_recv()
        made_ref[others[o]] = (
            arrived[others[o]].astype(jnp.float32) * inverse_ref[...]
        ).astype(jnp.bfloat16)

    everything.wait_send()
    for o in range(groups - 1):
        for part in range(2):
            @pl.when(direct(o, part))
            def _():
                cell_copy(o, part).wait_send()

    if detour:
        @pl.when((g == last) & (first == 0))
        def _():
            pass_copy().wait_send()

        @pl.when((g == RELAY) & (first == 0))
        def _():
            forward_copy().wait_send()

    @pl.when(d < columns - 1)
    def _():
        for o in range(groups):
            tail_copy(o).wait_send()


def finish(
    corrected_ref, made_ref, origin_ref, spill_ref, weights_ref,
    corrected_hbm, pooled_hbm,
    pooled_ref, sems, pooled_sem,
):
    tiles, planes, _ = corrected_ref.shape
    half_step = (COLS - OVL) // 2
    bf16, f32 = jnp.bfloat16, jnp.float32

    stores = [
        pltpu.make_async_copy(corrected_ref.at[t], corrected_hbm.at[t], sems.at[t])
        for t in range(tiles)
    ]
    for copy in stores:
        copy.start()
    where = origin_ref[...]
    origin = [where[j, 0] for j in range(tiles)]
    blocks = tiles * half_step // LANES
    pieces = [[] for _ in range(blocks + 1)]
    even = list(range(0, tiles, 2))
    odd = list(range(1, tiles, 2))

    def pool(kind, low_row, rows, windows):
        parts = []
        for which, base in windows:
            for j in which:
                parts.append(jnp.concatenate([
                    made_ref[origin[j], :, row * COLS + base:row * COLS + base + rows]
                    for row in range(ROWS)
                ], axis=1))
        total = jnp.dot(
            jnp.concatenate(parts, axis=0), weights_ref[kind, 0:ROWS * rows, :],
            preferred_element_type=f32,
        ).astype(bf16).astype(f32)
        i = 0
        for which, base in windows:
            for j in which:
                at = (2 * j * half_step + base - low_row) // BLOCK
                pieces[at].append(total[i * planes:(i + 1) * planes])
                i += 1

    pool(0, 0, BLOCK, [(even, 0)])
    pool(2, 0, BLOCK, [(even, COLS - BLOCK)])
    pool(3, OVL, BLOCK - OVL, [(odd, 0)])
    pool(4, 0, OVL, [(odd, COLS - OVL)])
    pool(1, 0, BLOCK, [(even, base) for base in range(BLOCK, COLS - BLOCK, BLOCK)]
         + [(odd, base) for base in range(OVL, COLS - OVL, BLOCK)])

    spill = jnp.dot(
        jnp.concatenate([spill_ref[row] for row in range(ROWS)], axis=1),
        weights_ref[4, 0:ROWS * OVL, :], preferred_element_type=f32,
    )
    pieces[0].append(spill.astype(bf16).astype(f32))
    for at in range(blocks):
        total = pieces[at][0]
        for piece in pieces[at][1:]:
            total = total + piece
        pooled_ref[:, at * LANES:(at + 1) * LANES] = total.astype(bf16)
    copy = pltpu.make_async_copy(pooled_ref, pooled_hbm, pooled_sem)
    copy.start()
    for done in stores + [copy]:
        done.wait()


def per_device(groups, columns, raw, dark, basis, counts, positions):
    tiles, planes, pixels = raw.shape
    rank = basis.shape[0]
    half_step = (COLS - OVL) // 2
    bf16, f32 = jnp.bfloat16, jnp.float32
    vmem = pl.BlockSpec(memory_space=pltpu.VMEM)
    anywhere = pl.BlockSpec(memory_space=pl.ANY)
    dma = pltpu.SemaphoreType.DMA
    passed = pl.pallas_call(
        functools.partial(gather, groups, columns),
        out_shape=(
            jax.ShapeDtypeStruct(raw.shape, bf16),
            jax.ShapeDtypeStruct((groups, planes, pixels), bf16),
            jax.ShapeDtypeStruct((tiles, LANES), jnp.int32),
            jax.ShapeDtypeStruct((ROWS, planes, OVL), bf16),
            jax.ShapeDtypeStruct((len(WINDOWS), ROWS * BLOCK, LANES), bf16),
        ),
        in_specs=[anywhere] * 5,
        out_specs=[vmem] * 5,
        scratch_shapes=[
            pltpu.SMEM(counts.shape, jnp.int32),
            pltpu.SMEM(positions.shape, jnp.int32),
            pltpu.VMEM((tiles, planes, HEAD), bf16),
            pltpu.VMEM((tiles, planes, pixels - HEAD), bf16),
            pltpu.VMEM(dark.shape, bf16),
            pltpu.VMEM((16, pixels), bf16),
            pltpu.VMEM((planes, LANES), f32),
            pltpu.VMEM((2, LANES), f32),
            pltpu.VMEM((groups * columns - 1, 2, LANES), f32),
            pltpu.VMEM((groups, planes, pixels), bf16),
            pltpu.VMEM((groups, planes, pixels), bf16),
            pltpu.VMEM((planes, HEAD), bf16),
            pltpu.VMEM((groups, ROWS, planes, OVL), bf16),
            pltpu.VMEM((groups, ROWS, planes, OVL), bf16),
            pltpu.VMEM(raw.shape, f32),
            pltpu.VMEM((planes * rank, pixels), bf16),
            pltpu.VMEM((planes, pixels), f32),
            dma((4,)), dma((2,)), pltpu.SemaphoreType.REGULAR,
            dma(()), dma(()),
            dma((2, groups)), dma((2, groups)), dma((groups,)), dma((groups,)),
            dma(()), dma(()), dma(()),
        ],
        compiler_params=pltpu.CompilerParams(
            collective_id=0, has_side_effects=True, vmem_limit_bytes=24 << 20
        ),
    )(*[pltpu.with_memory_space_constraint(x, pltpu.HBM) for x in (counts, positions, raw, dark, basis)])
    corrected, pooled = pl.pallas_call(
        finish,
        out_shape=(
            jax.ShapeDtypeStruct(raw.shape, bf16),
            jax.ShapeDtypeStruct((planes, tiles * half_step), bf16),
        ),
        in_specs=[vmem] * 5,
        out_specs=(anywhere, anywhere),
        scratch_shapes=[
            pltpu.VMEM((planes, tiles * half_step), bf16),
            dma((tiles,)), dma(()),
        ],
        compiler_params=pltpu.CompilerParams(vmem_limit_bytes=8 << 20),
    )(*passed)
    return corrected, pooled.reshape(1, planes, ROWS // 2, tiles * half_step)


def solution(mesh):
    in_specs = (P(("grp", "dev"), None, None), P(), P(), P(("grp", "dev")), P())
    out_specs = (P(("grp", "dev"), None, None), P("grp", None, None, "dev"))
    return jax.shard_map(
        functools.partial(per_device, mesh.shape["grp"], mesh.shape["dev"]),
        mesh=mesh, in_specs=in_specs, out_specs=out_specs, check_vma=False,
    )
```

```python
import functools

import jax
import jax.numpy as jnp
from jax import lax
from jax.experimental import pallas as pl
from jax.experimental.pallas import tpu as pltpu
from jax.sharding import PartitionSpec as P

ROWS = 2
COLS = 2048
OVL = 128
LANES = 128
BLOCK = 256
PAIR = 2
HEAD = 1152
RELAY = 1
MESH = pl.DeviceIdType.MESH
NT = (((1,), (1,)), ((), ()))


def pick(options):
    found = jnp.int32(0)
    for hit, value in options:
        found = jnp.where(hit, value, found)
    return found


def pool_weights(start):
    row = lax.broadcasted_iota(jnp.int32, (BLOCK, LANES), 0)
    lane = lax.broadcasted_iota(jnp.int32, (BLOCK, LANES), 1)
    column = (row + start).astype(jnp.float32) + 0.5
    ramp = jnp.minimum(1.0, jnp.minimum(column / OVL, (COLS - column) / OVL))
    inside = (row >= 2 * lane) & (row < 2 * lane + 2)
    return jnp.where(inside, 0.25 * jnp.maximum(ramp, 0.0), 0.0).astype(jnp.bfloat16)


WINDOWS = (
    (0, 0, BLOCK), (BLOCK, 0, BLOCK), (COLS - BLOCK, 0, BLOCK),
    (-OVL, OVL, BLOCK - OVL), (COLS - OVL, 0, OVL),
)


def gather(
    groups, columns,
    counts_hbm, positions_hbm, raw_hbm, dark_hbm, basis_hbm,
    corrected_ref, made_ref, origin_ref, spill_ref, weights_ref,
    counts_ref, positions_ref, raw_head, raw_rest, dark_ref, rhs, stat, mine, inbox, outgoing, arrived, passing, tail_out, tail_in,
    own_ref, stack_ref, inverse_ref,
    in_sem, raw_sem, above, stat_send, stat_recv, cell_send, cell_recv, tail_send, tail_recv,
    pass_send, pass_recv, forward_send,
):
    tiles, planes, pixels = raw_hbm.shape
    rank = basis_hbm.shape[0]
    band_size = columns * tiles
    devices = groups * columns
    g = lax.axis_index("grp")
    d = lax.axis_index("dev")
    first = lax.div(d, PAIR) * PAIR
    me = d * groups + g

    parts = [slice(0, HEAD), slice(HEAD, pixels)]
    early = [
        pltpu.make_async_copy(raw_hbm.at[:, :, parts[0]], raw_head, raw_sem.at[0]),
        pltpu.make_async_copy(counts_hbm, counts_ref, in_sem.at[0]),
        pltpu.make_async_copy(positions_hbm, positions_ref, in_sem.at[1]),
        pltpu.make_async_copy(dark_hbm, dark_ref, in_sem.at[2]),
    ]
    later = [
        pltpu.make_async_copy(basis_hbm, rhs.at[0:rank], in_sem.at[3]),
        pltpu.make_async_copy(raw_hbm.at[:, :, parts[1]], raw_rest, raw_sem.at[1]),
    ]
    for copy in early + later:
        copy.start()

    barrier = pltpu.get_barrier_semaphore()
    layer = [
        (lax.rem(g + a, groups), first + lax.rem(d - first + b, PAIR))
        for b in range(PAIR) for a in range(groups) if a or b
    ]
    for where in layer:
        pl.semaphore_signal(barrier, inc=1, device_id=where, device_id_type=MESH)

    @pl.loop(first + PAIR, columns)
    def _(column):
        for a in range(groups):
            pl.semaphore_signal(
                barrier, inc=1, device_id=(jnp.int32(a), column), device_id_type=MESH
            )

    rhs[rank:, :] = jnp.ones((rhs.shape[0] - rank, pixels), jnp.bfloat16)
    width = rhs.shape[0]
    stat[...] = jnp.zeros_like(stat)
    for copy in early:
        copy.wait()

    def home(at):
        return lax.div(at, band_size), lax.rem(at, tiles)

    depth = lax.broadcasted_iota(jnp.int32, (planes, LANES), 0)

    def alive(t):
        return jnp.where(depth < counts_ref[t], 1.0, 0.0).astype(jnp.bfloat16)

    def live(t):
        return jnp.concatenate([alive(t)] * (pixels // LANES), axis=1)

    def live_part(t, part):
        raw = (raw_head, raw_rest)[part][t]
        return (raw - dark_ref[:, parts[part]]) * live(t)[:, parts[part]]

    mine_home = [home(positions_ref[(g * columns + d) * tiles + t]) for t in range(tiles)]

    def build(b, part):
        chosen = pick((mine_home[t][0] == b, t) for t in range(tiles))
        outgoing[b, :, parts[part]] = live_part(chosen, part)

    def build_tail(b):
        chosen = pick((mine_home[t][0] == b, t) for t in range(tiles))
        for row in range(ROWS):
            span = slice((row + 1) * COLS - OVL, (row + 1) * COLS)
            raw = raw_rest[chosen, :, span.start - HEAD:span.stop - HEAD]
            tail_out[b, row] = (raw - dark_ref[:, span]) * alive(chosen)

    others = [jnp.where(g <= o, o + 1, o) for o in range(groups - 1)]

    def cell_copy(o, part):
        return pltpu.make_async_remote_copy(
            src_ref=outgoing.at[others[o], :, parts[part]], dst_ref=arrived.at[g, :, parts[part]],
            send_sem=cell_send.at[part, o], recv_sem=cell_recv.at[part, g],
            device_id=(others[o], d), device_id_type=MESH,
        )

    last = groups - 1
    detour = groups > RELAY + 2

    def pass_copy():
        return pltpu.make_async_remote_copy(
            src_ref=outgoing.at[0, :, parts[0]], dst_ref=passing,
            send_sem=pass_send, recv_sem=pass_recv,
            device_id=(jnp.int32(RELAY), d), device_id_type=MESH,
        )

    def forward_copy():
        return pltpu.make_async_remote_copy(
            src_ref=passing, dst_ref=arrived.at[last, :, parts[0]],
            send_sem=forward_send, recv_sem=cell_recv.at[0, last],
            device_id=(jnp.int32(0), d), device_id_type=MESH,
        )

    def direct(o, part):
        return ((g != last) | (first > 0)) if detour and o == 0 and part == 0 else (g >= 0)

    def tail_copy(o):
        other = lax.rem(g + o, groups)
        return pltpu.make_async_remote_copy(
            src_ref=tail_out.at[other], dst_ref=tail_in.at[g],
            send_sem=tail_send.at[o], recv_sem=tail_recv.at[g],
            device_id=(other, lax.rem(d + 1, columns)), device_id_type=MESH,
        )

    for o in range(groups - 1):
        build(others[o], 0)
    pl.semaphore_wait(barrier, (first + PAIR) * groups - 1)

    @pl.loop(0, first)
    def _(column):
        for a in range(groups):
            pl.semaphore_signal(above, inc=1, device_id=(jnp.int32(a), column), device_id_type=MESH)

    if detour:
        @pl.when((g == last) & (first == 0))
        def _():
            pass_copy().start()

    for o in range(groups - 1):
        @pl.when(direct(o, 0))
        def _():
            cell_copy(o, 0).start()

    for copy in later:
        copy.wait()

    raw = jnp.concatenate([raw_head[...], raw_rest[...]], axis=2)
    lhs = jnp.concatenate([raw.reshape(tiles * planes, pixels), dark_ref[...]], axis=0)
    sums = lax.dot_general(lhs, rhs[...], NT, preferred_element_type=jnp.float32)
    dark_sums = sums[tiles * planes:]
    plane = lax.broadcasted_iota(jnp.int32, (planes, width), 0)
    local = jnp.zeros((planes, width), jnp.float32)
    for t in range(tiles):
        part = sums[t * planes:(t + 1) * planes] - dark_sums
        local = local + jnp.where(plane < counts_ref[t], part, 0.0)
    stat[:, 0:width] = local
    lane = lax.broadcasted_iota(jnp.int32, (planes, LANES), 1)
    for i, turned in enumerate((stat[...], pltpu.roll(stat[...], LANES - rank, 1))):
        kept = jnp.where(lane < rank, turned, 0.0)
        spread = pltpu.roll(kept, 0, 1, stride=rank, stride_axis=0)
        mine[i:i + 1, :] = jnp.sum(spread, axis=0, keepdims=True)

    def stat_copy(a, column):
        slot = lax.rem(me - (column * groups + a) + devices, devices) - 1
        return pltpu.make_async_remote_copy(
            src_ref=mine, dst_ref=inbox.at[slot], send_sem=stat_send, recv_sem=stat_recv,
            device_id=(a, column), device_id_type=MESH,
        )

    @pl.loop(0, first)
    def _(column):
        for a in range(groups):
            stat_copy(jnp.int32(a), column).start()

    for a, column in layer:
        stat_copy(a, column).start()

    for b in range(groups):
        build_tail(b)

    build(others[0], 1)
    cell_copy(0, 1).start()

    @pl.when(d == first)
    def _():
        for o in range(groups):
            tail_copy(o).start()

    for o in range(groups - 2, 0, -1):
        build(others[o], 1)
        if detour and o == 1:
            @pl.when((g != RELAY) | (first > 0))
            def _():
                cell_copy(1, 1).start()
        else:
            cell_copy(o, 1).start()
    for part in range(2):
        build(g, part)

    for p in range(planes):
        stack_ref[p * rank:(p + 1) * rank, :] = rhs[0:rank, :]
    for i, (start, low, rows) in enumerate(WINDOWS):
        for row in range(ROWS):
            weights_ref[i, row * rows:(row + 1) * rows, :] = pool_weights(start)[low:low + rows]
    if detour:
        @pl.when((g == RELAY) & (first == 0))
        def _():
            pass_copy().wait_recv()
            forward_copy().start()
            cell_copy(1, 1).start()

    for t in range(tiles):
        bare = raw[t].astype(jnp.float32) - dark_ref[...].astype(jnp.float32)
        own_ref[t] = bare * live(t).astype(jnp.float32)

    there = [
        [home(positions_ref[(s * columns + d) * tiles + t]) for t in range(tiles)]
        for s in range(groups)
    ]
    slots = [
        pick((band == g, slot) for band, slot in there[s]) for s in range(groups)
    ]

    @pl.when(first + PAIR < columns)
    def _():
        pl.semaphore_wait(above, (columns - first - PAIR) * groups)

    @pl.loop(first + PAIR, columns)
    def _(column):
        for a in range(groups):
            stat_copy(jnp.int32(a), column).start()

    @pl.when((d > first) & (d < columns - 1))
    def _():
        for o in range(groups):
            tail_copy(o).start()

    everything = pltpu.make_async_remote_copy(
        src_ref=inbox, dst_ref=inbox, send_sem=stat_send, recv_sem=stat_recv,
        device_id=layer[0], device_id_type=MESH,
    )
    everything.wait_recv()
    sums = jnp.sum(inbox[...], axis=0) + mine[...]
    ratio = jnp.broadcast_to(sums[0:1, :] / sums[1:2, :], (planes, LANES))
    plane = lax.broadcasted_iota(jnp.int32, (planes, LANES), 0)
    lane = lax.broadcasted_iota(jnp.int32, (planes, LANES), 1)
    coef = jnp.where(lane // rank == plane, ratio, 0.0)
    high = coef.astype(jnp.bfloat16)
    rest = coef - high.astype(jnp.float32)
    middle = rest.astype(jnp.bfloat16)
    low = (rest - middle.astype(jnp.float32)).astype(jnp.bfloat16)
    split = jnp.concatenate([low, middle, high], axis=0)

    for block in range(pixels // BLOCK):
        span = slice(block * BLOCK, (block + 1) * BLOCK)
        shades = jnp.dot(split, stack_ref[:, span], preferred_element_type=jnp.float32)
        shade = shades[0:planes] + shades[planes:2 * planes] + shades[2 * planes:]
        inverse = jnp.exp(-shade)
        inverse_ref[:, span] = inverse
        for t in range(tiles):
            corrected_ref[t, :, span] = (own_ref[t, :, span] * inverse).astype(jnp.bfloat16)
    made_ref[g] = (outgoing[g].astype(jnp.float32) * inverse_ref[...]).astype(jnp.bfloat16)
    for j in range(tiles):
        origin = pick((slots[s] == j, s) for s in range(groups))
        origin_ref[j:j + 1, :] = jnp.full((1, LANES), origin, jnp.int32)

    spill_ref[...] = jnp.zeros_like(spill_ref)

    @pl.when(d > 0)
    def _():
        for o in range(groups):
            source = lax.rem(g + groups - o, groups)
            pltpu.make_async_remote_copy(
                src_ref=tail_out.at[source], dst_ref=tail_in.at[source],
                send_sem=tail_send.at[o], recv_sem=tail_recv.at[source],
                device_id=(source, lax.rem(d + columns - 1, columns)), device_id_type=MESH,
            ).wait_recv()
        before = [
            [home(positions_ref[(s * columns + d - 1) * tiles + t]) for t in range(tiles)]
            for s in range(groups)
        ]
        final = pick(
            ((band == g) & (slot == tiles - 1), s)
            for s in range(groups) for band, slot in before[s]
        )
        for row in range(ROWS):
            span = slice((row + 1) * COLS - OVL, (row + 1) * COLS)
            spill_ref[row] = (
                tail_in[final, row].astype(jnp.float32) * inverse_ref[:, span]
            ).astype(jnp.bfloat16)

    for o in range(groups - 1):
        for part in range(2):
            pltpu.make_async_remote_copy(
                src_ref=outgoing.at[others[o], :, parts[part]],
                dst_ref=arrived.at[others[o], :, parts[part]],
                send_sem=cell_send.at[part, o], recv_sem=cell_recv.at[part, others[o]],
                device_id=(others[o], d), device_id_type=MESH,
            ).wait_recv()
        made_ref[others[o]] = (
            arrived[others[o]].astype(jnp.float32) * inverse_ref[...]
        ).astype(jnp.bfloat16)

    everything.wait_send()
    for o in range(groups - 1):
        for part in range(2):
            @pl.when(direct(o, part))
            def _():
                cell_copy(o, part).wait_send()

    if detour:
        @pl.when((g == last) & (first == 0))
        def _():
            pass_copy().wait_send()

        @pl.when((g == RELAY) & (first == 0))
        def _():
            forward_copy().wait_send()

    @pl.when(d < columns - 1)
    def _():
        for o in range(groups):
            tail_copy(o).wait_send()


def finish(
    corrected_ref, made_ref, origin_ref, spill_ref, weights_ref,
    corrected_hbm, pooled_hbm,
    pooled_ref, sems, pooled_sem,
):
    tiles, planes, _ = corrected_ref.shape
    half_step = (COLS - OVL) // 2
    bf16, f32 = jnp.bfloat16, jnp.float32

    stores = [
        pltpu.make_async_copy(corrected_ref.at[t], corrected_hbm.at[t], sems.at[t])
        for t in range(tiles)
    ]
    for copy in stores:
        copy.start()
    where = origin_ref[...]
    origin = [where[j, 0] for j in range(tiles)]
    blocks = tiles * half_step // LANES
    pieces = [[] for _ in range(blocks + 1)]
    even = list(range(0, tiles, 2))
    odd = list(range(1, tiles, 2))

    def pool(kind, low_row, rows, windows):
        parts = []
        for which, base in windows:
            for j in which:
                parts.append(jnp.concatenate([
                    made_ref[origin[j], :, row * COLS + base:row * COLS + base + rows]
                    for row in range(ROWS)
                ], axis=1))
        total = jnp.dot(
            jnp.concatenate(parts, axis=0), weights_ref[kind, 0:ROWS * rows, :],
            preferred_element_type=f32,
        ).astype(bf16).astype(f32)
        i = 0
        for which, base in windows:
            for j in which:
                at = (2 * j * half_step + base - low_row) // BLOCK
                pieces[at].append(total[i * planes:(i + 1) * planes])
                i += 1

    pool(0, 0, BLOCK, [(even, 0)])
    pool(2, 0, BLOCK, [(even, COLS - BLOCK)])
    pool(3, OVL, BLOCK - OVL, [(odd, 0)])
    pool(4, 0, OVL, [(odd, COLS - OVL)])
    pool(1, 0, BLOCK, [(even, base) for base in range(BLOCK, COLS - BLOCK, BLOCK)]
         + [(odd, base) for base in range(OVL, COLS - OVL, BLOCK)])

    spill = jnp.dot(
        jnp.concatenate([spill_ref[row] for row in range(ROWS)], axis=1),
        weights_ref[4, 0:ROWS * OVL, :], preferred_element_type=f32,
    )
    pieces[0].append(spill.astype(bf16).astype(f32))
    for at in range(blocks):
        total = pieces[at][0]
        for piece in pieces[at][1:]:
            total = total + piece
        pooled_ref[:, at * LANES:(at + 1) * LANES] = total.astype(bf16)
    copy = pltpu.make_async_copy(pooled_ref, pooled_hbm, pooled_sem)
    copy.start()
    for done in stores + [copy]:
        done.wait()


def per_device(groups, columns, raw, dark, basis, counts, positions):
    tiles, planes, pixels = raw.shape
    rank = basis.shape[0]
    half_step = (COLS - OVL) // 2
    bf16, f32 = jnp.bfloat16, jnp.float32
    vmem = pl.BlockSpec(memory_space=pltpu.VMEM)
    anywhere = pl.BlockSpec(memory_space=pl.ANY)
    dma = pltpu.SemaphoreType.DMA
    passed = pl.pallas_call(
        functools.partial(gather, groups, columns),
        out_shape=(
            jax.ShapeDtypeStruct(raw.shape, bf16),
            jax.ShapeDtypeStruct((groups, planes, pixels), bf16),
            jax.ShapeDtypeStruct((tiles, LANES), jnp.int32),
            jax.ShapeDtypeStruct((ROWS, planes, OVL), bf16),
            jax.ShapeDtypeStruct((len(WINDOWS), ROWS * BLOCK, LANES), bf16),
        ),
        in_specs=[anywhere] * 5,
        out_specs=[vmem] * 5,
        scratch_shapes=[
            pltpu.SMEM(counts.shape, jnp.int32),
            pltpu.SMEM(positions.shape, jnp.int32),
            pltpu.VMEM((tiles, planes, HEAD), bf16),
            pltpu.VMEM((tiles, planes, pixels - HEAD), bf16),
            pltpu.VMEM(dark.shape, bf16),
            pltpu.VMEM((16, pixels), bf16),
            pltpu.VMEM((planes, LANES), f32),
            pltpu.VMEM((2, LANES), f32),
            pltpu.VMEM((groups * columns - 1, 2, LANES), f32),
            pltpu.VMEM((groups, planes, pixels), bf16),
            pltpu.VMEM((groups, planes, pixels), bf16),
            pltpu.VMEM((planes, HEAD), bf16),
            pltpu.VMEM((groups, ROWS, planes, OVL), bf16),
            pltpu.VMEM((groups, ROWS, planes, OVL), bf16),
            pltpu.VMEM(raw.shape, f32),
            pltpu.VMEM((planes * rank, pixels), bf16),
            pltpu.VMEM((planes, pixels), f32),
            dma((4,)), dma((2,)), pltpu.SemaphoreType.REGULAR,
            dma(()), dma(()),
            dma((2, groups)), dma((2, groups)), dma((groups,)), dma((groups,)),
            dma(()), dma(()), dma(()),
        ],
        compiler_params=pltpu.CompilerParams(
            collective_id=0, has_side_effects=True, vmem_limit_bytes=24 << 20
        ),
    )(*[pltpu.with_memory_space_constraint(x, pltpu.HBM) for x in (counts, positions, raw, dark, basis)])
    corrected, pooled = pl.pallas_call(
        finish,
        out_shape=(
            jax.ShapeDtypeStruct(raw.shape, bf16),
            jax.ShapeDtypeStruct((planes, tiles * half_step), bf16),
        ),
        in_specs=[vmem] * 5,
        out_specs=(anywhere, anywhere),
        scratch_shapes=[
            pltpu.VMEM((planes, tiles * half_step), bf16),
            dma((tiles,)), dma(()),
        ],
        compiler_params=pltpu.CompilerParams(vmem_limit_bytes=8 << 20),
    )(*passed)
    return corrected, pooled.reshape(1, planes, ROWS // 2, tiles * half_step)


def solution(mesh):
    in_specs = (P(("grp", "dev"), None, None), P(), P(), P(("grp", "dev")), P())
    out_specs = (P(("grp", "dev"), None, None), P("grp", None, None, "dev"))
    return jax.shard_map(
        functools.partial(per_device, mesh.shape["grp"], mesh.shape["dev"]),
        mesh=mesh, in_specs=in_specs, out_specs=out_specs, check_vma=False,
    )
```

```python
import functools

import jax
import jax.numpy as jnp
from jax import lax
from jax.experimental import pallas as pl
from jax.experimental.pallas import tpu as pltpu
from jax.sharding import PartitionSpec as P

ROWS = 2
COLS = 2048
OVL = 128
LANES = 128
BLOCK = 256
PAIR = 2
HEAD = 1152
RELAY = 1
MESH = pl.DeviceIdType.MESH
NT = (((1,), (1,)), ((), ()))


def pick(options):
    found = jnp.int32(0)
    for hit, value in options:
        found = jnp.where(hit, value, found)
    return found


def pool_weights(start):
    row = lax.broadcasted_iota(jnp.int32, (BLOCK, LANES), 0)
    lane = lax.broadcasted_iota(jnp.int32, (BLOCK, LANES), 1)
    column = (row + start).astype(jnp.float32) + 0.5
    ramp = jnp.minimum(1.0, jnp.minimum(column / OVL, (COLS - column) / OVL))
    inside = (row >= 2 * lane) & (row < 2 * lane + 2)
    return jnp.where(inside, 0.25 * jnp.maximum(ramp, 0.0), 0.0).astype(jnp.bfloat16)


WINDOWS = (
    (0, 0, BLOCK, 0, BLOCK),
    (1, 0, 0, 0, BLOCK), (1, 1, COLS - BLOCK, 0, BLOCK),
    (2, 0, -OVL, OVL, BLOCK - OVL), (2, 1, COLS - OVL, 0, OVL),
)


def gather(
    groups, columns,
    counts_hbm, positions_hbm, raw_hbm, dark_hbm, basis_hbm,
    corrected_ref, made_ref, origin_ref, spill_ref, weights_ref,
    counts_ref, positions_ref, raw_head, raw_rest, dark_ref, rhs, stat, mine, inbox, outgoing, arrived, passing, tail_out, tail_in,
    own_ref, stack_ref, inverse_ref,
    in_sem, raw_sem, above, stat_send, stat_recv, cell_send, cell_recv, tail_send, tail_recv,
    pass_send, pass_recv, forward_send,
):
    tiles, planes, pixels = raw_hbm.shape
    rank = basis_hbm.shape[0]
    band_size = columns * tiles
    devices = groups * columns
    g = lax.axis_index("grp")
    d = lax.axis_index("dev")
    first = lax.div(d, PAIR) * PAIR
    me = d * groups + g

    parts = [slice(0, HEAD), slice(HEAD, pixels)]
    early = [
        pltpu.make_async_copy(raw_hbm.at[:, :, parts[0]], raw_head, raw_sem.at[0]),
        pltpu.make_async_copy(counts_hbm, counts_ref, in_sem.at[0]),
        pltpu.make_async_copy(positions_hbm, positions_ref, in_sem.at[1]),
        pltpu.make_async_copy(dark_hbm, dark_ref, in_sem.at[2]),
    ]
    later = [
        pltpu.make_async_copy(basis_hbm, rhs.at[0:rank], in_sem.at[3]),
        pltpu.make_async_copy(raw_hbm.at[:, :, parts[1]], raw_rest, raw_sem.at[1]),
    ]
    for copy in early + later:
        copy.start()

    barrier = pltpu.get_barrier_semaphore()
    layer = [
        (lax.rem(g + a, groups), first + lax.rem(d - first + b, PAIR))
        for b in range(PAIR) for a in range(groups) if a or b
    ]
    for where in layer:
        pl.semaphore_signal(barrier, inc=1, device_id=where, device_id_type=MESH)

    @pl.loop(first + PAIR, columns)
    def _(column):
        for a in range(groups):
            pl.semaphore_signal(
                barrier, inc=1, device_id=(jnp.int32(a), column), device_id_type=MESH
            )

    rhs[rank:, :] = jnp.ones((rhs.shape[0] - rank, pixels), jnp.bfloat16)
    width = rhs.shape[0]
    stat[...] = jnp.zeros_like(stat)
    for copy in early:
        copy.wait()

    def home(at):
        return lax.div(at, band_size), lax.rem(at, tiles)

    depth = lax.broadcasted_iota(jnp.int32, (planes, LANES), 0)

    def alive(t):
        return jnp.where(depth < counts_ref[t], 1.0, 0.0).astype(jnp.bfloat16)

    def live(t):
        return jnp.concatenate([alive(t)] * (pixels // LANES), axis=1)

    def live_part(t, part):
        raw = (raw_head, raw_rest)[part][t]
        return (raw - dark_ref[:, parts[part]]) * live(t)[:, parts[part]]

    mine_home = [home(positions_ref[(g * columns + d) * tiles + t]) for t in range(tiles)]

    def build(b, part):
        chosen = pick((mine_home[t][0] == b, t) for t in range(tiles))
        outgoing[b, :, parts[part]] = live_part(chosen, part)

    def build_tail(b):
        chosen = pick((mine_home[t][0] == b, t) for t in range(tiles))
        for row in range(ROWS):
            span = slice((row + 1) * COLS - OVL, (row + 1) * COLS)
            raw = raw_rest[chosen, :, span.start - HEAD:span.stop - HEAD]
            tail_out[b, row] = (raw - dark_ref[:, span]) * alive(chosen)

    others = [jnp.where(g <= o, o + 1, o) for o in range(groups - 1)]

    def cell_copy(o, part):
        return pltpu.make_async_remote_copy(
            src_ref=outgoing.at[others[o], :, parts[part]], dst_ref=arrived.at[g, :, parts[part]],
            send_sem=cell_send.at[part, o], recv_sem=cell_recv.at[part, g],
            device_id=(others[o], d), device_id_type=MESH,
        )

    last = groups - 1
    detour = groups > RELAY + 2

    def pass_copy():
        return pltpu.make_async_remote_copy(
            src_ref=outgoing.at[0, :, parts[0]], dst_ref=passing,
            send_sem=pass_send, recv_sem=pass_recv,
            device_id=(jnp.int32(RELAY), d), device_id_type=MESH,
        )

    def forward_copy():
        return pltpu.make_async_remote_copy(
            src_ref=passing, dst_ref=arrived.at[last, :, parts[0]],
            send_sem=forward_send, recv_sem=cell_recv.at[0, last],
            device_id=(jnp.int32(0), d), device_id_type=MESH,
        )

    def direct(o, part):
        return ((g != last) | (first > 0)) if detour and o == 0 and part == 0 else (g >= 0)

    def tail_copy(o):
        other = lax.rem(g + o, groups)
        return pltpu.make_async_remote_copy(
            src_ref=tail_out.at[other], dst_ref=tail_in.at[g],
            send_sem=tail_send.at[o], recv_sem=tail_recv.at[g],
            device_id=(other, lax.rem(d + 1, columns)), device_id_type=MESH,
        )

    for o in range(groups - 1):
        build(others[o], 0)
    pl.semaphore_wait(barrier, (first + PAIR) * groups - 1)

    @pl.loop(0, first)
    def _(column):
        for a in range(groups):
            pl.semaphore_signal(above, inc=1, device_id=(jnp.int32(a), column), device_id_type=MESH)

    if detour:
        @pl.when((g == last) & (first == 0))
        def _():
            pass_copy().start()

    for o in range(groups - 1):
        @pl.when(direct(o, 0))
        def _():
            cell_copy(o, 0).start()

    for copy in later:
        copy.wait()

    raw = jnp.concatenate([raw_head[...], raw_rest[...]], axis=2)
    lhs = jnp.concatenate([raw.reshape(tiles * planes, pixels), dark_ref[...]], axis=0)
    sums = lax.dot_general(lhs, rhs[...], NT, preferred_element_type=jnp.float32)
    dark_sums = sums[tiles * planes:]
    plane = lax.broadcasted_iota(jnp.int32, (planes, width), 0)
    local = jnp.zeros((planes, width), jnp.float32)
    for t in range(tiles):
        part = sums[t * planes:(t + 1) * planes] - dark_sums
        local = local + jnp.where(plane < counts_ref[t], part, 0.0)
    stat[:, 0:width] = local
    lane = lax.broadcasted_iota(jnp.int32, (planes, LANES), 1)
    for i, turned in enumerate((stat[...], pltpu.roll(stat[...], LANES - rank, 1))):
        kept = jnp.where(lane < rank, turned, 0.0)
        spread = pltpu.roll(kept, 0, 1, stride=rank, stride_axis=0)
        mine[i:i + 1, :] = jnp.sum(spread, axis=0, keepdims=True)

    def stat_copy(a, column):
        slot = lax.rem(me - (column * groups + a) + devices, devices) - 1
        return pltpu.make_async_remote_copy(
            src_ref=mine, dst_ref=inbox.at[slot], send_sem=stat_send, recv_sem=stat_recv,
            device_id=(a, column), device_id_type=MESH,
        )

    @pl.loop(0, first)
    def _(column):
        for a in range(groups):
            stat_copy(jnp.int32(a), column).start()

    for a, column in layer:
        stat_copy(a, column).start()

    for b in range(groups):
        build_tail(b)

    build(others[0], 1)
    cell_copy(0, 1).start()

    for o in range(groups - 2, 0, -1):
        build(others[o], 1)
        if o == 1:
            @pl.when(d == first)
            def _():
                for p in range(groups):
                    tail_copy(p).start()

        if detour and o == 1:
            @pl.when((g != RELAY) | (first > 0))
            def _():
                cell_copy(1, 1).start()
        else:
            cell_copy(o, 1).start()
    for part in range(2):
        build(g, part)

    for p in range(planes):
        stack_ref[p * rank:(p + 1) * rank, :] = rhs[0:rank, :]
    for i, side, start, low, rows in WINDOWS:
        lanes = slice(side * LANES, (side + 1) * LANES)
        for row in range(ROWS):
            weights_ref[i, row * rows:(row + 1) * rows, lanes] = pool_weights(start)[low:low + rows]
    if detour:
        @pl.when((g == RELAY) & (first == 0))
        def _():
            pass_copy().wait_recv()
            forward_copy().start()
            cell_copy(1, 1).start()

    for t in range(tiles):
        bare = raw[t].astype(jnp.float32) - dark_ref[...].astype(jnp.float32)
        own_ref[t] = bare * live(t).astype(jnp.float32)

    there = [
        [home(positions_ref[(s * columns + d) * tiles + t]) for t in range(tiles)]
        for s in range(groups)
    ]
    slots = [
        pick((band == g, slot) for band, slot in there[s]) for s in range(groups)
    ]

    @pl.when(first + PAIR < columns)
    def _():
        pl.semaphore_wait(above, (columns - first - PAIR) * groups)

    @pl.loop(first + PAIR, columns)
    def _(column):
        for a in range(groups):
            stat_copy(jnp.int32(a), column).start()

    @pl.when((d > first) & (d < columns - 1))
    def _():
        for o in range(groups):
            tail_copy(o).start()

    everything = pltpu.make_async_remote_copy(
        src_ref=inbox, dst_ref=inbox, send_sem=stat_send, recv_sem=stat_recv,
        device_id=layer[0], device_id_type=MESH,
    )
    everything.wait_recv()
    sums = jnp.sum(inbox[...], axis=0) + mine[...]
    ratio = jnp.broadcast_to(sums[0:1, :] / sums[1:2, :], (planes, LANES))
    plane = lax.broadcasted_iota(jnp.int32, (planes, LANES), 0)
    lane = lax.broadcasted_iota(jnp.int32, (planes, LANES), 1)
    coef = jnp.where(lane // rank == plane, ratio, 0.0)
    high = coef.astype(jnp.bfloat16)
    rest = coef - high.astype(jnp.float32)
    middle = rest.astype(jnp.bfloat16)
    low = (rest - middle.astype(jnp.float32)).astype(jnp.bfloat16)
    split = jnp.concatenate([low, middle, high], axis=0)

    for block in range(pixels // BLOCK):
        span = slice(block * BLOCK, (block + 1) * BLOCK)
        shades = jnp.dot(split, stack_ref[:, span], preferred_element_type=jnp.float32)
        shade = shades[0:planes] + shades[planes:2 * planes] + shades[2 * planes:]
        inverse = jnp.exp(-shade)
        inverse_ref[:, span] = inverse
        for t in range(tiles):
            corrected_ref[t, :, span] = (own_ref[t, :, span] * inverse).astype(jnp.bfloat16)
    made_ref[g] = (outgoing[g].astype(jnp.float32) * inverse_ref[...]).astype(jnp.bfloat16)
    for j in range(tiles):
        origin = pick((slots[s] == j, s) for s in range(groups))
        origin_ref[j:j + 1, :] = jnp.full((1, LANES), origin, jnp.int32)

    spill_ref[...] = jnp.zeros_like(spill_ref)

    @pl.when(d > 0)
    def _():
        for o in range(groups):
            source = lax.rem(g + groups - o, groups)
            pltpu.make_async_remote_copy(
                src_ref=tail_out.at[source], dst_ref=tail_in.at[source],
                send_sem=tail_send.at[o], recv_sem=tail_recv.at[source],
                device_id=(source, lax.rem(d + columns - 1, columns)), device_id_type=MESH,
            ).wait_recv()
        before = [
            [home(positions_ref[(s * columns + d - 1) * tiles + t]) for t in range(tiles)]
            for s in range(groups)
        ]
        final = pick(
            ((band == g) & (slot == tiles - 1), s)
            for s in range(groups) for band, slot in before[s]
        )
        for row in range(ROWS):
            span = slice((row + 1) * COLS - OVL, (row + 1) * COLS)
            spill_ref[row] = (
                tail_in[final, row].astype(jnp.float32) * inverse_ref[:, span]
            ).astype(jnp.bfloat16)

    for o in range(groups - 1):
        for part in range(2):
            pltpu.make_async_remote_copy(
                src_ref=outgoing.at[others[o], :, parts[part]],
                dst_ref=arrived.at[others[o], :, parts[part]],
                send_sem=cell_send.at[part, o], recv_sem=cell_recv.at[part, others[o]],
                device_id=(others[o], d), device_id_type=MESH,
            ).wait_recv()
        made_ref[others[o]] = (
            arrived[others[o]].astype(jnp.float32) * inverse_ref[...]
        ).astype(jnp.bfloat16)

    everything.wait_send()
    for o in range(groups - 1):
        for part in range(2):
            @pl.when(direct(o, part))
            def _():
                cell_copy(o, part).wait_send()

    if detour:
        @pl.when((g == last) & (first == 0))
        def _():
            pass_copy().wait_send()

        @pl.when((g == RELAY) & (first == 0))
        def _():
            forward_copy().wait_send()

    @pl.when(d < columns - 1)
    def _():
        for o in range(groups):
            tail_copy(o).wait_send()


def finish(
    corrected_ref, made_ref, origin_ref, spill_ref, weights_ref,
    corrected_hbm, pooled_hbm,
    pooled_ref, sems, pooled_sem,
):
    tiles, planes, _ = corrected_ref.shape
    half_step = (COLS - OVL) // 2
    bf16, f32 = jnp.bfloat16, jnp.float32

    stores = [
        pltpu.make_async_copy(corrected_ref.at[t], corrected_hbm.at[t], sems.at[t])
        for t in range(tiles)
    ]
    for copy in stores:
        copy.start()
    where = origin_ref[...]
    origin = [where[j, 0] for j in range(tiles)]
    blocks = tiles * half_step // LANES
    pieces = [[] for _ in range(blocks + 1)]
    even = list(range(0, tiles, 2))
    odd = list(range(1, tiles, 2))

    def side_by_side(rows, windows):
        return [
            jnp.concatenate([
                made_ref[origin[j], :, row * COLS + base:row * COLS + base + rows]
                for row in range(ROWS)
            ], axis=1)
            for which, base in windows for j in which
        ]

    def pool(parts, weights):
        total = jnp.dot(jnp.concatenate(parts, axis=0), weights, preferred_element_type=f32)
        return total.astype(bf16).astype(f32)

    def put(total, low_row, windows, sides):
        i = 0
        for (which, base), side in zip(windows, sides):
            lanes = slice(side * LANES, (side + 1) * LANES)
            for j in which:
                at = (2 * j * half_step + base - low_row) // BLOCK
                pieces[at].append(total[i * planes:(i + 1) * planes, lanes])
                i += 1

    ends = [(even, 0), (even, COLS - BLOCK)]
    put(pool(side_by_side(BLOCK, ends), weights_ref[1]), 0, ends, (0, 1))
    spill = jnp.concatenate([spill_ref[row] for row in range(ROWS)], axis=1)
    total = pool(
        side_by_side(OVL, [(odd, 0), (odd, COLS - OVL)]) + [spill], weights_ref[2, 0:ROWS * OVL, :]
    )
    count = len(odd) * planes
    put(total[0:count], OVL, [(odd, 0)], (0,))
    put(total[count:2 * count], 0, [(odd, COLS - OVL)], (1,))
    pieces[0].append(total[2 * count:, LANES:])
    inner = [(even, base) for base in range(BLOCK, COLS - BLOCK, BLOCK)]
    inner += [(odd, base) for base in range(OVL, COLS - OVL, BLOCK)]
    put(pool(side_by_side(BLOCK, inner), weights_ref[0, :, 0:LANES]), 0, inner, [0] * len(inner))

    for at in range(blocks):
        total = pieces[at][0]
        for piece in pieces[at][1:]:
            total = total + piece
        pooled_ref[:, at * LANES:(at + 1) * LANES] = total.astype(bf16)
    copy = pltpu.make_async_copy(pooled_ref, pooled_hbm, pooled_sem)
    copy.start()
    for done in stores + [copy]:
        done.wait()


def per_device(groups, columns, raw, dark, basis, counts, positions):
    tiles, planes, pixels = raw.shape
    rank = basis.shape[0]
    half_step = (COLS - OVL) // 2
    bf16, f32 = jnp.bfloat16, jnp.float32
    vmem = pl.BlockSpec(memory_space=pltpu.VMEM)
    anywhere = pl.BlockSpec(memory_space=pl.ANY)
    dma = pltpu.SemaphoreType.DMA
    passed = pl.pallas_call(
        functools.partial(gather, groups, columns),
        out_shape=(
            jax.ShapeDtypeStruct(raw.shape, bf16),
            jax.ShapeDtypeStruct((groups, planes, pixels), bf16),
            jax.ShapeDtypeStruct((tiles, LANES), jnp.int32),
            jax.ShapeDtypeStruct((ROWS, planes, OVL), bf16),
            jax.ShapeDtypeStruct((3, ROWS * BLOCK, 2 * LANES), bf16),
        ),
        in_specs=[anywhere] * 5,
        out_specs=[vmem] * 5,
        scratch_shapes=[
            pltpu.SMEM(counts.shape, jnp.int32),
            pltpu.SMEM(positions.shape, jnp.int32),
            pltpu.VMEM((tiles, planes, HEAD), bf16),
            pltpu.VMEM((tiles, planes, pixels - HEAD), bf16),
            pltpu.VMEM(dark.shape, bf16),
            pltpu.VMEM((16, pixels), bf16),
            pltpu.VMEM((planes, LANES), f32),
            pltpu.VMEM((2, LANES), f32),
            pltpu.VMEM((groups * columns - 1, 2, LANES), f32),
            pltpu.VMEM((groups, planes, pixels), bf16),
            pltpu.VMEM((groups, planes, pixels), bf16),
            pltpu.VMEM((planes, HEAD), bf16),
            pltpu.VMEM((groups, ROWS, planes, OVL), bf16),
            pltpu.VMEM((groups, ROWS, planes, OVL), bf16),
            pltpu.VMEM(raw.shape, f32),
            pltpu.VMEM((planes * rank, pixels), bf16),
            pltpu.VMEM((planes, pixels), f32),
            dma((4,)), dma((2,)), pltpu.SemaphoreType.REGULAR,
            dma(()), dma(()),
            dma((2, groups)), dma((2, groups)), dma((groups,)), dma((groups,)),
            dma(()), dma(()), dma(()),
        ],
        compiler_params=pltpu.CompilerParams(
            collective_id=0, has_side_effects=True, vmem_limit_bytes=24 << 20
        ),
    )(*[pltpu.with_memory_space_constraint(x, pltpu.HBM) for x in (counts, positions, raw, dark, basis)])
    corrected, pooled = pl.pallas_call(
        finish,
        out_shape=(
            jax.ShapeDtypeStruct(raw.shape, bf16),
            jax.ShapeDtypeStruct((planes, tiles * half_step), bf16),
        ),
        in_specs=[vmem] * 5,
        out_specs=(anywhere, anywhere),
        scratch_shapes=[
            pltpu.VMEM((planes, tiles * half_step), bf16),
            dma((tiles,)), dma(()),
        ],
        compiler_params=pltpu.CompilerParams(vmem_limit_bytes=8 << 20),
    )(*passed)
    return corrected, pooled.reshape(1, planes, ROWS // 2, tiles * half_step)


def solution(mesh):
    in_specs = (P(("grp", "dev"), None, None), P(), P(), P(("grp", "dev")), P())
    out_specs = (P(("grp", "dev"), None, None), P("grp", None, None, "dev"))
    return jax.shard_map(
        functools.partial(per_device, mesh.shape["grp"], mesh.shape["dev"]),
        mesh=mesh, in_specs=in_specs, out_specs=out_specs, check_vma=False,
    )
```
